768 devices in a mesh: item: 32 (over x, y_lo, core), split: 24 (over y_hi, z).
Axes of the slice: x: 4, y: 8 (y_hi: 2, y_lo: 4; y = y_hi * 4 + y_lo), z: 12, core: 2. Of those that a mesh axis runs over, the one named last changes fastest.
Arguments:
- item_emb: float32 [16384, 128], P('item'), may hold values from -0.046875 to 0.046875
- confidences: bfloat16 [32, 24, 4, 16, 8, 128], P('item', 'split'), may hold values from 1 to 64
- user_block: int32 [32, 24, 4, 16], P('item', 'split'), may hold values from 0 to 2
- item_block: int32 [32, 24, 4, 16], P('item', 'split'), may hold values from 0 to 3
- block_age: int32 [32, 24, 4, 16], P('item', 'split'), may hold values from 0 to 15
- block_count: int32 [32, 24, 4], P('item', 'split'), may hold values from 8 to 16, as said below
Outputs:
- user_emb: float32 [768, 128], P('item')
The draws below stay inside these ranges and needn't reach their ends.
Inputs may be any that keep to these rules, and one draw needn't show every extreme that they name: `block_count`: every device has 16 live slots at some window offset in some draw; some device has them in every draw.
All inputs are finite; a program needn't handle non-finite values.
Results may differ from the reference program's by a relative error of at most 0.0003.
Values sent between devices are 32-bit elements; how exact they have to be, the bound alone decides.
A program may use at most 32 MiB of HBM per device.

```python
import math
import jax
import jax.numpy as jnp
from jax import lax

EMB = 128
BLOCK_ITEMS = 128
BLOCK_USERS = 8
USER_BLOCKS = 3
ITEM_BLOCKS = 4
BLK_STEP = 16
STEPS = 4
CG_ITERS = 3
ITEM_ROWS = 512
ITEMS = 16384
USERS_DEV = 24
USERS = 768
N_ITEM = 32
N_SPLIT = 24


def draw_block_count(key, part):
    key_drop, key_chosen = jax.random.split(key, 2)
    drop = jax.random.randint(key_drop, (N_ITEM, N_SPLIT, STEPS), 0, max(2, BLK_STEP // 2 + 1))
    counts = BLK_STEP - drop
    chosen = jax.random.randint(key_chosen, (), 0, N_ITEM * N_SPLIT * STEPS)
    flattened = counts.reshape(-1).at[chosen].set(BLK_STEP)
    return flattened.reshape(N_ITEM, N_SPLIT, STEPS).astype(jnp.int32)


def with_ends(drawn, stream_key, low, high):
    extent = drawn.shape
    index_at = [jax.random.randint(jax.random.fold_in(stream_key, axis), (), 0, extent[axis]) for axis in range(len(extent))]
    drawn = drawn.at[tuple(index_at)].set(low)
    longest = extent.index(max(extent))
    index_at[longest] = (index_at[longest] + 1) % extent[longest]
    return drawn.at[tuple(index_at)].set(high)


def level_of(rng, dims, shards, low, top_value):
    gain = 1.0
    for axis_at, blocks in shards:
        draws = jax.random.uniform(jax.random.fold_in(jax.random.fold_in(rng, 6), axis_at), (blocks,), jnp.float32, low / len(shards), top_value / len(shards))
        gain = gain * jnp.repeat(jnp.exp(draws), dims[axis_at] // blocks).reshape((-1,) + (1,) * (len(dims) - 1 - axis_at))
    return gain


def normal_values(key, extent, scale, reach, cuts=(), kind=jnp.bfloat16):
    array = scale * jax.random.normal(key, extent, jnp.float32)
    if cuts:
        array = array * level_of(key, extent, cuts, -0.22, 0.18)
    return jnp.clip(array, -reach, reach).astype(kind)


def setup_inputs(seed: int = 0) -> dict:
    arg_keys = jax.random.split(jax.random.key(seed), 7)
    return {
        "item_emb": normal_values(arg_keys[0], (ITEMS, EMB), ITEMS ** -0.5, 0.046875, ((0, 32),), jnp.float32),
        "confidences": jnp.clip(jnp.exp(math.log(64.0) - 4.158883 * jax.random.uniform(arg_keys[1], (N_ITEM, N_SPLIT, STEPS, BLK_STEP, BLOCK_USERS, BLOCK_ITEMS), jnp.float32) ** level_of(arg_keys[1], (N_ITEM, N_SPLIT, STEPS, BLK_STEP, BLOCK_USERS, BLOCK_ITEMS), ((0, 32), (1, 24)), -0.2, 0.2)), 1.0, 64.0).astype(jnp.bfloat16),
        "user_block": with_ends(jax.random.randint(arg_keys[2], (N_ITEM, N_SPLIT, STEPS, BLK_STEP), 0, USER_BLOCKS), jax.random.fold_in(arg_keys[2], 1), 0, USER_BLOCKS - 1).astype(jnp.int32),
        "item_block": with_ends(jax.random.randint(arg_keys[3], (N_ITEM, N_SPLIT, STEPS, BLK_STEP), 0, ITEM_BLOCKS), jax.random.fold_in(arg_keys[3], 1), 0, ITEM_BLOCKS - 1).astype(jnp.int32),
        "block_age": with_ends(jax.random.randint(arg_keys[4], (N_ITEM, N_SPLIT, STEPS, BLK_STEP), 0, 16), jax.random.fold_in(arg_keys[4], 1), 0, 15).astype(jnp.int32),
        "block_count": draw_block_count(jax.random.fold_in(arg_keys[6], 71), 0),
    }


ridge_weight = 0.1


def conjugate(matrix, right):
    solution = jnp.zeros_like(right)
    residual = right
    direction = right
    norm_now = jnp.sum(residual * residual, axis=1)
    for iteration in range(CG_ITERS):
        image = jnp.einsum('ude,ue->ud', matrix, direction, precision=lax.Precision.HIGHEST)
        step_size = norm_now / jnp.sum(direction * image, axis=1)
        solution = solution + step_size[:, None] * direction
        residual = residual - step_size[:, None] * image
        norm_next = jnp.sum(residual * residual, axis=1)
        direction = residual + (norm_next / norm_now)[:, None] * direction
        norm_now = norm_next
    return solution


def reference(item_emb, confidences, user_block, item_block, block_age, block_count):
    base = jnp.dot(item_emb.T, item_emb, precision=lax.Precision.HIGHEST, preferred_element_type=jnp.float32)
    base = base + ridge_weight * jnp.eye(EMB, dtype=jnp.float32)

    def solve_group(group):
        window = jnp.concatenate([lax.dynamic_slice_in_dim(item_emb, (((group - offset) % N_ITEM) * ITEM_ROWS).astype(jnp.int32), ITEM_ROWS, 0) for offset in range(STEPS)], axis=0)
        weights = lax.dynamic_index_in_dim(confidences, group, 0, keepdims=False).astype(jnp.float32)
        users_here = lax.dynamic_index_in_dim(user_block, group, 0, keepdims=False)
        items_here = lax.dynamic_index_in_dim(item_block, group, 0, keepdims=False)
        ages_here = lax.dynamic_index_in_dim(block_age, group, 0, keepdims=False)
        counts_here = lax.dynamic_index_in_dim(block_count, group, 0, keepdims=False)
        recency = 2.0 / (2.0 + ages_here.astype(jnp.float32))
        live = (jnp.arange(BLK_STEP, dtype=jnp.int32)[None, None, :] < counts_here[:, :, None]).astype(jnp.float32)
        factor = (recency * live)[..., None, None]
        conf_part = weights * factor
        pref_part = (weights + 1.0) * factor
        row_index = users_here[..., None, None] * BLOCK_USERS + jnp.arange(BLOCK_USERS, dtype=jnp.int32)[:, None]
        col_index = jnp.arange(STEPS, dtype=jnp.int32)[None, :, None, None, None] * ITEM_ROWS + items_here[..., None, None] * BLOCK_ITEMS + jnp.arange(BLOCK_ITEMS, dtype=jnp.int32)[None, :]
        row_index = jnp.broadcast_to(row_index, conf_part.shape)
        col_index = jnp.broadcast_to(col_index, conf_part.shape)
        conf_weight = jnp.zeros((USERS_DEV, STEPS * ITEM_ROWS), jnp.float32).at[row_index, col_index].add(conf_part)
        pref_weight = jnp.zeros((USERS_DEV, STEPS * ITEM_ROWS), jnp.float32).at[row_index, col_index].add(pref_part)
        system = jnp.einsum('ui,id,ie->ude', conf_weight, window, window, precision=lax.Precision.HIGHEST) + base[None]
        right = jnp.dot(pref_weight, window, precision=lax.Precision.HIGHEST, preferred_element_type=jnp.float32)
        return conjugate(system, right)

    solved = lax.map(solve_group, jnp.arange(N_ITEM, dtype=jnp.int32))
    return solved.reshape(USERS, EMB)
```

```python
import jax
import jax.numpy as jnp
from jax import lax
from jax.experimental import pallas as pl
from jax.experimental.pallas import tpu as pltpu
from jax.sharding import PartitionSpec as P

CG_ITERS = 3
STEPS = 4
SLOTS = 16
USERS = 24
EMB = 128
ROWS = 512
X, Y, C = 4, 4, 2
N_ITEM = X * Y * C
Z = 12
N_SPLIT = 2 * Z
NEAR = Y * C
CHUNKS = 2
CHUNK = ROWS // CHUNKS
RIDGE = 0.1
F32 = jnp.float32
BF16 = jnp.bfloat16
MESH = pl.DeviceIdType.MESH


def high_low(value):
    high = value.astype(BF16)
    return high, (value - high.astype(F32)).astype(BF16)


def block_weights(user_block, item_block, block_age, block_count):
    lane = lax.broadcasted_iota(jnp.int32, (STEPS, SLOTS), 1)
    row = lax.broadcasted_iota(jnp.int32, (STEPS, STEPS), 0)
    col = lax.broadcasted_iota(jnp.int32, (STEPS, STEPS), 1)
    counts = jnp.broadcast_to(block_count.astype(F32), (STEPS, STEPS))
    counts = jnp.sum(jnp.where(row == col, counts, 0.0), axis=1, keepdims=True)
    recency = 2.0 / (2.0 + block_age.astype(F32))
    recency = jnp.where(lane.astype(F32) < counts, recency, 0.0)
    code = (user_block * 4 + item_block).astype(F32)
    both = jnp.concatenate([recency, code], axis=0)
    slot = lax.broadcasted_iota(jnp.int32, (SLOTS, EMB), 0)
    spread = lax.broadcasted_iota(jnp.int32, (SLOTS, EMB), 1) // 8
    spread = jnp.where(slot == spread, 1.0, 0.0).astype(F32)
    return jnp.dot(both, spread, precision=lax.Precision.HIGHEST, preferred_element_type=F32)


def kernel(
    emb_ref, conf_ref, user_ref, item_ref, age_ref, count_ref, out_ref,
    send_a, recv_a, send_r, recv_r, pair_c, pair_r, recv_b, recv_s,
    window, window_t, split_w, local_gram, gram_1, gram_2, gram_3, result,
    sem_as, sem_ar, sem_rs, sem_rr, sem_bs, sem_br,
    sem_ws, sem_wr, sem_g1s, sem_g1r, sem_g2s, sem_g2r, sem_g3s, sem_g3r,
    sem_xs, sem_xr,
):
    item = lax.axis_index("item")
    split = lax.axis_index("split")
    core = lax.rem(item, C)
    near = lax.rem(item, NEAR)
    at_x = item // NEAR
    at_y = near // C
    y_hi = split // Z
    at_z = lax.rem(split, Z)
    other_y = 1 - y_hi
    partner = other_y * Z + at_z
    user = 2 * at_z + y_hi
    last_y = (at_y == Y - 1).astype(jnp.int32)
    first_y = (at_y == 0).astype(jnp.int32)
    next_split = (y_hi + last_y * (1 - 2 * y_hi)) * Z + at_z
    prev_split = (y_hi + first_y * (1 - 2 * y_hi)) * Z + at_z
    next_item = lax.rem(item + C, N_ITEM)
    prev_item = lax.rem(item + N_ITEM - C, N_ITEM)
    other_core = item + 1 - 2 * core

    def at_split(d):
        return lax.rem(split + d, N_SPLIT)

    def at_depth(d):
        return lax.rem(at_z + d, Z)

    def at_near(d):
        return lax.rem(near + d, NEAR)

    def at_far(d):
        return lax.rem(at_x + d, X)

    barrier = pltpu.get_barrier_semaphore()

    def greet(device):
        pl.semaphore_signal(barrier, inc=1, device_id=device, device_id_type=MESH)

    @pl.loop(1, N_SPLIT)
    def _(d):
        greet((item, at_split(d)))

    @pl.loop(1, NEAR)
    def _(d):
        greet((at_x * NEAR + at_near(d), split))

    @pl.loop(1, X)
    def _(d):
        greet((at_far(d) * NEAR + near, split))

    greet((next_item, next_split))
    greet((prev_item, prev_split))

    @pl.when(core == 1)
    def _():
        greet((lax.rem(item + 1, N_ITEM), next_split))

    @pl.when(core == 0)
    def _():
        greet((lax.rem(item + N_ITEM - 1, N_ITEM), prev_split))

    def copy(src, dst, send_sem, recv_sem, device):
        return pltpu.make_async_remote_copy(
            src_ref=src, dst_ref=dst, send_sem=send_sem, recv_sem=recv_sem,
            device_id=device, device_id_type=MESH,
        )

    spread = block_weights(user_ref[...], item_ref[...], age_ref[...], count_ref[...])
    half = USERS * 8
    row = lax.broadcasted_iota(jnp.int32, (half, 1), 0)
    row_user = row // 8
    row_code = ((row_user // 8) * 4 + lax.rem(row, 4)) * 16
    row_code = row_code + (lax.rem(row, 8) // 4) * 8 + lax.rem(row_user, 8)
    row_code = row_code.astype(F32)
    lane = lax.broadcasted_iota(jnp.int32, (1, 2 * EMB), 1)
    lane_code = (lane // EMB * 8 + lax.rem(lane, 8)).astype(F32)
    ones = jnp.ones((2 * EMB, EMB), BF16)
    rows_8 = lax.broadcasted_iota(jnp.int32, (8, EMB), 0)
    lanes_8 = lax.broadcasted_iota(jnp.int32, (8, EMB), 1)
    recency_rows = [jnp.zeros((1, EMB), F32) for _ in range(3)]
    for pair in range(2):
        k = 2 * pair
        recency = jnp.concatenate([spread[k : k + 1], spread[k + 1 : k + 2]], axis=1)
        code = jnp.concatenate([spread[4 + k : 5 + k], spread[5 + k : 6 + k]], axis=1)
        code = code * 16.0 + lane_code
        place = jnp.where(row_code == code, recency, 0.0)
        high, rest = high_low(place)
        low = (place - high.astype(F32) - rest.astype(F32)).astype(BF16)
        values = jnp.concatenate([conf_ref[pl.ds(2 * EMB * pair, 2 * EMB), :], ones], axis=1)
        sums = jnp.dot(
            jnp.concatenate([high, rest, low], axis=0), values, preferred_element_type=F32
        )
        sums = sums[:half] + sums[half : 2 * half] + sums[2 * half :]
        send_a[:, pl.ds(8 * pair, 8), :] = sums[:, :EMB].reshape(USERS, 8, EMB)
        for block in range(3):
            part = sums[64 * block : 64 * block + 8, EMB:]
            part = jnp.where(lanes_8 == rows_8 + 8 * pair, part, 0.0)
            recency_rows[block] = recency_rows[block] + jnp.sum(part, axis=0, keepdims=True)
    for block in range(3):
        send_r[block] = recency_rows[block]

    pl.semaphore_wait(barrier, N_SPLIT - 1 + NEAR - 1 + X - 1 + 3)

    def own_next(c):
        return copy(
            emb_ref.at[pl.ds(c * CHUNK, CHUNK)], window.at[2, pl.ds(c * CHUNK, CHUNK)],
            sem_ws.at[0, c], sem_wr.at[1, c], (next_item, next_split),
        )

    def own_core(c):
        return copy(
            emb_ref.at[pl.ds(c * CHUNK, CHUNK)], window.at[1, pl.ds(c * CHUNK, CHUNK)],
            sem_ws.at[1, c], sem_wr.at[0, c], (other_core, split),
        )

    def relay_core(c, slot, send_slot):
        return copy(
            window.at[2, pl.ds(c * CHUNK, CHUNK)], window.at[slot, pl.ds(c * CHUNK, CHUNK)],
            sem_ws.at[send_slot, c], sem_wr.at[slot - 1, c], (other_core, split),
        )

    def relay_next(c):
        return copy(
            window.at[2, pl.ds(c * CHUNK, CHUNK)], window.at[3, pl.ds(c * CHUNK, CHUNK)],
            sem_ws.at[2, c], sem_wr.at[2, c], (lax.rem(item + 1, N_ITEM), next_split),
        )

    for c in range(CHUNKS):
        own_next(c).start()

    def depth_copy(d):
        peer = at_depth(d)
        return copy(
            send_a.at[pl.ds(2 * peer, 2)], recv_a.at[at_z],
            sem_as.at[d], sem_ar.at[at_z], (item, y_hi * Z + peer),
        )

    def depth_copy_r(d):
        peer = at_depth(d)
        return copy(
            send_r.at[peer // 4], recv_r.at[at_z],
            sem_rs.at[d], sem_rr.at[at_z], (item, y_hi * Z + peer),
        )

    @pl.loop(1, Z)
    def _(d):
        depth_copy(d).start()
        depth_copy_r(d).start()

    @pl.when(core == 0)
    def _():
        for c in range(CHUNKS):
            own_core(c).start()

    def prepare(slot, rows):
        high, low = high_low(rows)
        split_w[slot, :, pl.ds(0, EMB)] = high
        split_w[slot, :, pl.ds(EMB, EMB)] = low
        turned = rows.T
        window_t[slot] = turned
        return turned

    def three_products(left, slot):
        high, low = high_low(left)
        count = left.shape[0]
        both = jnp.concatenate([high, low], axis=0)
        out = jnp.dot(both, split_w[slot], preferred_element_type=F32)
        return out[:count, :EMB] + out[:count, EMB:] + out[count:, :EMB]

    turned = prepare(0, emb_ref[...])
    local_gram[...] = three_products(turned, 0).reshape(NEAR, EMB // NEAR, EMB)

    def gram_copy_1(d):
        peer = at_near(d)
        return copy(
            local_gram.at[peer], gram_1.at[near],
            sem_g1s.at[d], sem_g1r.at[near], (at_x * NEAR + peer, split),
        )

    def gram_copy_2(d):
        peer = at_far(d)
        return copy(
            gram_2.at[at_x], gram_2.at[at_x],
            sem_g2s.at[d], sem_g2r.at[at_x], (peer * NEAR + near, split),
        )

    def gram_copy_3(d):
        peer = at_near(d)
        return copy(
            gram_3.at[near], gram_3.at[near],
            sem_g3s.at[d], sem_g3r.at[near], (at_x * NEAR + peer, split),
        )

    @pl.loop(1, NEAR)
    def _(d):
        gram_copy_1(d).start()

    for c in range(CHUNKS):
        own_next(c).wait_recv()

        @pl.when(core == 0)
        def _():
            relay_core(c, 3, 2).start()

        @pl.when(core == 1)
        def _():
            relay_next(c).start()
            relay_core(c, 1, 1).start()

    def sum_1(d, total):
        peer = at_near(d)
        copy(
            local_gram.at[peer], gram_1.at[peer], sem_g1s.at[d], sem_g1r.at[peer],
            (at_x * NEAR + peer, split),
        ).wait_recv()
        return total + gram_1[peer]

    gram_2[at_x] = lax.fori_loop(1, NEAR, sum_1, local_gram[near])

    @pl.loop(1, X)
    def _(d):
        gram_copy_2(d).start()

    def sum_z(d, totals):
        total, total_r = totals
        peer = at_depth(d)
        copy(
            send_a.at[pl.ds(0, 2)], recv_a.at[peer], sem_as.at[d], sem_ar.at[peer],
            (item, y_hi * Z + peer),
        ).wait_recv()
        copy(
            send_r.at[0], recv_r.at[peer], sem_rs.at[d], sem_rr.at[peer],
            (item, y_hi * Z + peer),
        ).wait_recv()
        return total + recv_a[peer], total_r + recv_r[peer]

    total, total_r = lax.fori_loop(
        1, Z, sum_z, (send_a[pl.ds(2 * at_z, 2)], send_r[at_z // 4])
    )
    pair_c[...] = total
    pair_r[...] = total_r
    send_pair = copy(
        pair_c.at[other_y], recv_b, sem_bs.at[0], sem_br.at[0], (item, partner)
    )
    send_pair_r = copy(pair_r, recv_s, sem_bs.at[1], sem_br.at[1], (item, partner))
    send_pair.start()
    send_pair_r.start()

    def sum_2(d, total):
        peer = at_far(d)
        copy(
            gram_2.at[peer], gram_2.at[peer], sem_g2s.at[d], sem_g2r.at[peer],
            (peer * NEAR + near, split),
        ).wait_recv()
        return total + gram_2[peer]

    gram_3[near] = lax.fori_loop(1, X, sum_2, gram_2[at_x])

    @pl.loop(1, NEAR)
    def _(d):
        gram_copy_3(d).start()

    prepare(2, window[2])
    send_pair.wait_recv()
    send_pair_r.wait_recv()
    weights = pair_c[y_hi] + recv_b[...]
    block_row = jnp.broadcast_to(pair_r[...] + recv_s[...], (SLOTS, EMB))
    rows_16 = lax.broadcasted_iota(jnp.int32, (SLOTS, EMB), 0)
    lanes_16 = lax.broadcasted_iota(jnp.int32, (SLOTS, EMB), 1)
    block_col = jnp.sum(jnp.where(rows_16 == lanes_16, block_row, 0.0), axis=1, keepdims=True)
    wishes = weights + block_col

    def weighted(slot):
        base = 4 * slot
        left = jnp.concatenate(
            [
                window_t[slot, :, pl.ds(b * EMB, EMB)] * weights[base + b : base + b + 1]
                for b in range(4)
            ],
            axis=1,
        )
        wish = jnp.concatenate([wishes[base + b : base + b + 1] for b in range(4)], axis=1)
        wish = jnp.broadcast_to(wish, (8, ROWS))
        return three_products(jnp.concatenate([left, wish], axis=0), slot)

    system = weighted(0) + weighted(2)
    for slot in (1, 3):
        for c in range(CHUNKS):
            copy(
                window.at[2, pl.ds(c * CHUNK, CHUNK)],
                window.at[slot, pl.ds(c * CHUNK, CHUNK)],
                sem_ws.at[0, c], sem_wr.at[slot - 1, c], (other_core, split),
            ).wait_recv()
        prepare(slot, window[slot])
        system = system + weighted(slot)

    @pl.loop(1, NEAR)
    def _(d):
        peer = at_near(d)
        copy(
            gram_3.at[peer], gram_3.at[peer], sem_g3s.at[d], sem_g3r.at[peer],
            (at_x * NEAR + peer, split),
        ).wait_recv()

    eye = lax.broadcasted_iota(jnp.int32, (EMB, EMB), 0)
    eye = eye == lax.broadcasted_iota(jnp.int32, (EMB, EMB), 1)
    base = gram_3[...].reshape(EMB, EMB) + jnp.where(eye, RIDGE, 0.0)
    matrix = system[:EMB] + base
    right = system[EMB:]

    def over(value):
        return jnp.sum(value, axis=1, keepdims=True)

    answer = jnp.zeros_like(right)
    residual = right
    direction = right
    norm_now = over(residual * residual)
    for _ in range(CG_ITERS):
        image = jnp.dot(
            direction, matrix, precision=lax.Precision.HIGHEST, preferred_element_type=F32
        )
        step_size = norm_now / over(direction * image)
        answer = answer + step_size * direction
        residual = residual - step_size * image
        norm_next = over(residual * residual)
        direction = residual + (norm_next / norm_now) * direction
        norm_now = norm_next
    result[user] = answer[:1]

    def answer_copy(d):
        return copy(
            result.at[user], result.at[user], sem_xs.at[d], sem_xr.at[split],
            (item, at_split(d)),
        )

    @pl.loop(1, N_SPLIT)
    def _(d):
        answer_copy(d).start()

    for c in range(CHUNKS):
        own_next(c).wait_send()
        relay_core(c, 1, 1).wait_send()
        relay_next(c).wait_send()

    @pl.loop(1, Z)
    def _(d):
        depth_copy(d).wait_send()
        depth_copy_r(d).wait_send()

    send_pair.wait_send()
    send_pair_r.wait_send()

    @pl.loop(1, NEAR)
    def _(d):
        gram_copy_1(d).wait_send()
        gram_copy_3(d).wait_send()

    @pl.loop(1, X)
    def _(d):
        gram_copy_2(d).wait_send()

    @pl.loop(1, N_SPLIT)
    def _(d):
        peer = at_split(d)
        row = 2 * lax.rem(peer, Z) + peer // Z
        copy(
            result.at[row], result.at[row], sem_xs.at[d], sem_xr.at[peer], (item, peer)
        ).wait_recv()

    @pl.loop(1, N_SPLIT)
    def _(d):
        answer_copy(d).wait_send()

    for u in range(USERS):
        out_ref[u : u + 1, :] = result[u]


def body(item_emb, confidences, user_block, item_block, block_age, block_count):
    dma = pltpu.SemaphoreType.DMA
    vmem = pl.BlockSpec(memory_space=pltpu.VMEM)
    return pl.pallas_call(
        kernel,
        out_shape=jax.ShapeDtypeStruct((USERS, EMB), F32),
        in_specs=[vmem] * 6,
        out_specs=vmem,
        scratch_shapes=[
            pltpu.VMEM((USERS, SLOTS, EMB), F32),
            pltpu.VMEM((Z, 2, SLOTS, EMB), F32),
            pltpu.VMEM((3, 1, EMB), F32),
            pltpu.VMEM((Z, 1, EMB), F32),
            pltpu.VMEM((2, SLOTS, EMB), F32),
            pltpu.VMEM((1, EMB), F32),
            pltpu.VMEM((SLOTS, EMB), F32),
            pltpu.VMEM((1, EMB), F32),
            pltpu.VMEM((STEPS, ROWS, EMB), F32),
            pltpu.VMEM((STEPS, EMB, ROWS), F32),
            pltpu.VMEM((STEPS, ROWS, 2 * EMB), BF16),
            pltpu.VMEM((NEAR, EMB // NEAR, EMB), F32),
            pltpu.VMEM((NEAR, EMB // NEAR, EMB), F32),
            pltpu.VMEM((X, EMB // NEAR, EMB), F32),
            pltpu.VMEM((NEAR, EMB // NEAR, EMB), F32),
            pltpu.VMEM((USERS, 1, EMB), F32),
            dma((Z,)), dma((Z,)), dma((Z,)), dma((Z,)), dma((2,)), dma((2,)),
            dma((3, CHUNKS)), dma((3, CHUNKS)),
            dma((NEAR,)), dma((NEAR,)), dma((X,)), dma((X,)), dma((NEAR,)), dma((NEAR,)),
            dma((N_SPLIT,)), dma((N_SPLIT,)),
        ],
        compiler_params=pltpu.CompilerParams(
            collective_id=0, has_side_effects=True, vmem_limit_bytes=32 << 20
        ),
        name="als_half_sweep",
    )(
        item_emb,
        confidences.reshape(ROWS, EMB),
        user_block.reshape(STEPS, SLOTS),
        item_block.reshape(STEPS, SLOTS),
        block_age.reshape(STEPS, SLOTS),
        block_count.reshape(1, STEPS),
    )


def solution(mesh):
    placed = (
        P("item", None),
        P("item", "split", None, None, None, None),
        P("item", "split", None, None),
        P("item", "split", None, None),
        P("item", "split", None, None),
        P("item", "split", None),
    )
    return jax.shard_map(
        body, mesh=mesh, in_specs=placed, out_specs=P("item", None), check_vma=False
    )
```

```python
import jax
import jax.numpy as jnp
from jax import lax
from jax.experimental import pallas as pl
from jax.experimental.pallas import tpu as pltpu
from jax.sharding import PartitionSpec as P

CG_ITERS = 3
STEPS = 4
SLOTS = 16
USERS = 24
EMB = 128
ROWS = 512
X, Y, C = 4, 4, 2
N_ITEM = X * Y * C
Z = 12
SIDE = X * C
BLOCK = EMB // SIDE
CHUNKS = 2
CHUNK = ROWS // CHUNKS
RIDGE = 0.1
HELD = 40
SENT = 33
FAR_FIRST = (6, 5, 7, 4, 8, 3, 9, 2, 10, 1, 11)
F32 = jnp.float32
BF16 = jnp.bfloat16
MESH = pl.DeviceIdType.MESH


def high_low(value):
    high = value.astype(BF16)
    return high, (value - high.astype(F32)).astype(BF16)


def block_weights(user_block, item_block, block_age, block_count):
    lane = lax.broadcasted_iota(jnp.int32, (STEPS, SLOTS), 1)
    row = lax.broadcasted_iota(jnp.int32, (STEPS, STEPS), 0)
    col = lax.broadcasted_iota(jnp.int32, (STEPS, STEPS), 1)
    counts = jnp.broadcast_to(block_count.astype(F32), (STEPS, STEPS))
    counts = jnp.sum(jnp.where(row == col, counts, 0.0), axis=1, keepdims=True)
    recency = 2.0 / (2.0 + block_age.astype(F32))
    recency = jnp.where(lane.astype(F32) < counts, recency, 0.0)
    code = (user_block * 4 + item_block).astype(F32)
    both = jnp.concatenate([recency, code], axis=0)
    slot = lax.broadcasted_iota(jnp.int32, (SLOTS, EMB), 0)
    spread = lax.broadcasted_iota(jnp.int32, (SLOTS, EMB), 1) // 8
    spread = jnp.where(slot == spread, 1.0, 0.0).astype(F32)
    return jnp.dot(both, spread, precision=lax.Precision.HIGHEST, preferred_element_type=F32)


def kernel(
    emb_hbm, conf_hbm, user_hbm, item_hbm, age_hbm, count_hbm, out_ref,
    emb_ref, conf_ref, user_ref, item_ref, age_ref, count_ref,
    send_a, recv_a, pair_a, recv_b,
    window, window_t, split_w, local_gram, gram_1, gram_2, gram_3, result,
    sem_in, sem_as, sem_ar, sem_bs, sem_br,
    sem_ws, sem_wr, sem_g1s, sem_g1r, sem_g2s, sem_g2r, sem_g3s, sem_g3r,
    sem_xs, sem_xr,
):
    item = lax.axis_index("item")
    split = lax.axis_index("split")
    core = lax.rem(item, C)
    at_x = item // (Y * C)
    at_y = lax.rem(item, Y * C) // C
    side = at_x * C + core
    y_hi = split // Z
    at_z = lax.rem(split, Z)
    partner = (1 - y_hi) * Z + at_z
    last_y = (at_y == Y - 1).astype(jnp.int32)
    first_y = (at_y == 0).astype(jnp.int32)
    next_split = (y_hi + last_y * (1 - 2 * y_hi)) * Z + at_z
    prev_split = (y_hi + first_y * (1 - 2 * y_hi)) * Z + at_z
    next_item = lax.rem(item + C, N_ITEM)
    prev_item = lax.rem(item + N_ITEM - C, N_ITEM)
    cross_next = lax.rem(item + 1, N_ITEM)
    cross_prev = lax.rem(item + N_ITEM - 1, N_ITEM)
    other_core = item + 1 - 2 * core

    def at_depth(d):
        return lax.rem(at_z + d, Z)

    def at_side(d):
        peer = lax.rem(side + d, SIDE)
        return peer, (peer // C * (Y * C) + at_y * C + lax.rem(peer, C), split)

    def along_y(d):
        place = lax.rem(y_hi * Y + at_y + d + 2 * Y, 2 * Y)
        at = lax.rem(place, Y)
        return at, (at_x * (Y * C) + at * C + core, place // Y * Z + at_z)

    barrier = pltpu.get_barrier_semaphore()

    def greet(device):
        pl.semaphore_signal(barrier, inc=1, device_id=device, device_id_type=MESH)

    for d in FAR_FIRST:
        greet((item, y_hi * Z + at_depth(d)))
    greet((item, partner))
    for d in (1, 2, 3, -1, -2, -3):
        greet(along_y(d)[1])
    for d in range(1, SIDE):
        greet(at_side(d)[1])
    greet((next_item, next_split))
    greet((prev_item, prev_split))

    @pl.when(core == 1)
    def _():
        greet((cross_next, next_split))

    @pl.when(core == 0)
    def _():
        greet((cross_prev, prev_split))

    loads = [
        pltpu.make_async_copy(src, dst, sem_in.at[n])
        for n, (src, dst) in enumerate(
            (
                (user_hbm, user_ref),
                (item_hbm, item_ref),
                (age_hbm, age_ref),
                (count_hbm, count_ref),
                (conf_hbm, conf_ref),
                (emb_hbm, emb_ref),
            )
        )
    ]
    for load in loads:
        load.start()

    def copy(src, dst, send_sem, recv_sem, device):
        return pltpu.make_async_remote_copy(
            src_ref=src, dst_ref=dst, send_sem=send_sem, recv_sem=recv_sem,
            device_id=device, device_id_type=MESH,
        )

    for load in loads[:4]:
        load.wait()
    spread = block_weights(user_ref[...], item_ref[...], age_ref[...], count_ref[...])
    half = USERS * 8
    row = lax.broadcasted_iota(jnp.int32, (half, 1), 0)
    row_user = row // 8
    row_code = ((row_user // 8) * 4 + lax.rem(row, 4)) * 16
    row_code = row_code + (lax.rem(row, 8) // 4) * 8 + lax.rem(row_user, 8)
    row_code = row_code.astype(F32)
    lane = lax.broadcasted_iota(jnp.int32, (1, 2 * EMB), 1)
    lane_code = (lane // EMB * 8 + lax.rem(lane, 8)).astype(F32)
    ones = jnp.ones((2 * EMB, EMB), BF16)
    rows_8 = lax.broadcasted_iota(jnp.int32, (8, EMB), 0)
    lanes_8 = lax.broadcasted_iota(jnp.int32, (8, EMB), 1)
    recency_rows = [jnp.zeros((1, EMB), F32) for _ in range(3)]
    loads[4].wait()
    for pair in range(2):
        k = 2 * pair
        recency = jnp.concatenate([spread[k : k + 1], spread[k + 1 : k + 2]], axis=1)
        code = jnp.concatenate([spread[4 + k : 5 + k], spread[5 + k : 6 + k]], axis=1)
        code = code * 16.0 + lane_code
        place = jnp.where(row_code == code, recency, 0.0)
        high, rest = high_low(place)
        low = (place - high.astype(F32) - rest.astype(F32)).astype(BF16)
        values = jnp.concatenate([conf_ref[pl.ds(2 * EMB * pair, 2 * EMB), :], ones], axis=1)
        sums = jnp.dot(
            jnp.concatenate([high, rest, low], axis=0), values, preferred_element_type=F32
        )
        sums = sums[:half] + sums[half : 2 * half] + sums[2 * half :]
        by_user = sums[:, :EMB].reshape(Z, 2, 8, EMB)
        for u in range(2):
            send_a[:, pl.ds(SLOTS * u + 8 * pair, 8), :] = by_user[:, u]
        for block in range(3):
            part = sums[64 * block : 64 * block + 8, EMB:]
            part = jnp.where(lanes_8 == rows_8 + 8 * pair, part, 0.0)
            recency_rows[block] = recency_rows[block] + jnp.sum(part, axis=0, keepdims=True)
    for peer in range(Z):
        send_a[peer, 2 * SLOTS : 2 * SLOTS + 1, :] = recency_rows[peer // 4]

    def prepare(slot, rows):
        high, low = high_low(rows)
        split_w[slot, :, pl.ds(0, EMB)] = high
        split_w[slot, :, pl.ds(EMB, EMB)] = low
        turned = rows.T
        window_t[slot] = turned
        return turned

    def three_products(left, slot):
        high, low = high_low(left)
        count = left.shape[0]
        both = jnp.concatenate([high, low], axis=0)
        out = jnp.dot(both, split_w[slot], preferred_element_type=F32)
        return out[:count, :EMB] + out[:count, EMB:] + out[count:, :EMB]

    loads[5].wait()
    turned = prepare(0, emb_ref[...])
    local_gram[...] = three_products(turned, 0).reshape(SIDE, BLOCK, EMB)

    pl.semaphore_wait(barrier, Z - 1 + 1 + 6 + SIDE - 1 + 3)

    def chunk(c):
        return pl.ds(c * CHUNK, CHUNK)

    def own_next(c):
        return copy(
            emb_ref.at[chunk(c)], window.at[2, chunk(c)],
            sem_ws.at[0, c], sem_wr.at[1, c], (next_item, next_split),
        )

    def own_core(c):
        return copy(
            emb_ref.at[chunk(c)], window.at[1, chunk(c)],
            sem_ws.at[1, c], sem_wr.at[0, c], (other_core, split),
        )

    def relay_core(c, slot, send_slot):
        return copy(
            window.at[2, chunk(c)], window.at[slot, chunk(c)],
            sem_ws.at[send_slot, c], sem_wr.at[slot - 1, c], (other_core, split),
        )

    def relay_next(c):
        return copy(
            window.at[2, chunk(c)], window.at[3, chunk(c)],
            sem_ws.at[2, c], sem_wr.at[2, c], (cross_next, next_split),
        )

    def pass_on(c):
        own_next(c).wait_recv()

        @pl.when(core == 1)
        def _():
            relay_next(c).start()

    def share(c):
        @pl.when(core == 0)
        def _():
            relay_core(c, 3, 2).start()

        @pl.when(core == 1)
        def _():
            relay_core(c, 1, 1).start()

    def depth_copy(d):
        peer = at_depth(d)
        return copy(
            send_a.at[peer, pl.ds(0, SENT)], recv_a.at[at_z, pl.ds(0, SENT)],
            sem_as.at[d], sem_ar.at[at_z], (item, y_hi * Z + peer),
        )

    def gram_copy_1(d):
        peer, device = at_side(d)
        return copy(
            local_gram.at[peer], gram_1.at[side], sem_g1s.at[d], sem_g1r.at[side], device
        )

    def gram_copy_2(n, d):
        return copy(
            gram_2.at[at_y], gram_2.at[at_y], sem_g2s.at[n], sem_g2r.at[at_y], along_y(d)[1]
        )

    def gram_copy_3(d):
        return copy(
            gram_3.at[side], gram_3.at[side], sem_g3s.at[d], sem_g3r.at[side], at_side(d)[1]
        )

    for d in FAR_FIRST:
        depth_copy(d).start()
    for d in range(1, SIDE):
        gram_copy_1(d).start()
    for c in range(CHUNKS):
        own_next(c).start()

    @pl.when(core == 0)
    def _():
        for c in range(CHUNKS):
            own_core(c).start()

    def sum_z(d, total):
        peer = at_depth(d)
        copy(
            send_a.at[0, pl.ds(0, SENT)], recv_a.at[peer, pl.ds(0, SENT)],
            sem_as.at[d], sem_ar.at[peer], (item, y_hi * Z + peer),
        ).wait_recv()
        return total + recv_a[peer, pl.ds(0, SENT)]

    pair_a[pl.ds(0, SENT)] = lax.fori_loop(1, Z, sum_z, send_a[at_z, pl.ds(0, SENT)])
    send_pair = copy(
        pair_a.at[pl.ds(0, SENT)], recv_b.at[pl.ds(0, SENT)], sem_bs, sem_br, (item, partner)
    )
    send_pair.start()

    total = local_gram[side]
    for d in range(1, SIDE):
        peer, device = at_side(d)
        copy(
            local_gram.at[peer], gram_1.at[peer], sem_g1s.at[d], sem_g1r.at[peer], device
        ).wait_recv()
        total = total + gram_1[peer]
    gram_2[at_y] = total
    for n, d in enumerate((-3, -2, -1)):
        gram_copy_2(n, d).start()

    for c in range(CHUNKS):
        pass_on(c)
        share(c)
    prepare(2, window[2])
    for n, d in enumerate((3, 2, 1)):
        at, device = along_y(d)
        copy(
            gram_2.at[at], gram_2.at[at], sem_g2s.at[n], sem_g2r.at[at], device
        ).wait_recv()
    gram_3[side] = gram_2[0] + gram_2[1] + gram_2[2] + gram_2[3]
    for d in range(1, SIDE):
        gram_copy_3(d).start()

    for slot in (1, 3):
        for c in range(CHUNKS):
            copy(
                window.at[2, chunk(c)], window.at[slot, chunk(c)],
                sem_ws.at[0, c], sem_wr.at[slot - 1, c], (other_core, split),
            ).wait_recv()
        prepare(slot, window[slot])
    for d in range(1, SIDE):
        peer, device = at_side(d)
        copy(
            gram_3.at[peer], gram_3.at[peer], sem_g3s.at[d], sem_g3r.at[peer], device
        ).wait_recv()
    eye = lax.broadcasted_iota(jnp.int32, (EMB, EMB), 0)
    eye = eye == lax.broadcasted_iota(jnp.int32, (EMB, EMB), 1)
    base = gram_3[...].reshape(EMB, EMB) + jnp.where(eye, RIDGE, 0.0)

    send_pair.wait_recv()
    both = pair_a[pl.ds(0, SENT)] + recv_b[pl.ds(0, SENT)]
    weights = both[: 2 * SLOTS].reshape(2, SLOTS, EMB)
    block_row = jnp.broadcast_to(both[2 * SLOTS : 2 * SLOTS + 1], (SLOTS, EMB))
    rows_16 = lax.broadcasted_iota(jnp.int32, (SLOTS, EMB), 0)
    lanes_16 = lax.broadcasted_iota(jnp.int32, (SLOTS, EMB), 1)
    block_col = jnp.sum(jnp.where(rows_16 == lanes_16, block_row, 0.0), axis=1, keepdims=True)

    def weighted(slot):
        base_row = 4 * slot
        parts = []
        for u in range(2):
            wishes = weights[u] + block_col
            parts.append(
                jnp.concatenate(
                    [
                        window_t[slot, :, pl.ds(b * EMB, EMB)]
                        * weights[u, base_row + b : base_row + b + 1]
                        for b in range(4)
                    ],
                    axis=1,
                )
            )
            wish = jnp.concatenate(
                [wishes[base_row + b : base_row + b + 1] for b in range(4)], axis=1
            )
            parts.append(jnp.broadcast_to(wish, (8, ROWS)))
        return three_products(jnp.concatenate(parts, axis=0), slot)

    system = weighted(0)
    for slot in range(1, STEPS):
        system = system + weighted(slot)

    def over(value):
        return jnp.sum(value, axis=1, keepdims=True)

    stride = EMB + 8
    matrices = [system[u * stride : u * stride + EMB] + base for u in range(2)]
    right = jnp.concatenate(
        [system[u * stride + EMB : (u + 1) * stride] for u in range(2)], axis=0
    )
    answer = jnp.zeros_like(right)
    residual = right
    direction = right
    norm_now = over(residual * residual)
    for _ in range(CG_ITERS):
        image = jnp.concatenate(
            [
                jnp.dot(
                    direction[8 * u : 8 * u + 8], matrices[u],
                    precision=lax.Precision.HIGHEST, preferred_element_type=F32,
                )
                for u in range(2)
            ],
            axis=0,
        )
        step_size = norm_now / over(direction * image)
        answer = answer + step_size * direction
        residual = residual - step_size * image
        norm_next = over(residual * residual)
        direction = residual + (norm_next / norm_now) * direction
        norm_now = norm_next
    result[2 * at_z] = answer[:1]
    result[2 * at_z + 1] = answer[8:9]

    def answer_copy(d):
        return copy(
            result.at[pl.ds(2 * at_z, 2)], result.at[pl.ds(2 * at_z, 2)],
            sem_xs.at[d], sem_xr.at[at_z], (item, y_hi * Z + at_depth(d)),
        )

    for d in FAR_FIRST:
        answer_copy(d).start()

    for c in range(CHUNKS):
        own_next(c).wait_send()
        relay_core(c, 1, 1).wait_send()
        relay_next(c).wait_send()
    for d in range(1, Z):
        depth_copy(d).wait_send()
    send_pair.wait_send()
    for d in range(1, SIDE):
        gram_copy_1(d).wait_send()
        gram_copy_3(d).wait_send()
    for n, d in enumerate((-3, -2, -1)):
        gram_copy_2(n, d).wait_send()
    for d in range(1, Z):
        peer = at_depth(d)
        copy(
            result.at[pl.ds(2 * peer, 2)], result.at[pl.ds(2 * peer, 2)],
            sem_xs.at[d], sem_xr.at[peer], (item, y_hi * Z + peer),
        ).wait_recv()
    for d in range(1, Z):
        answer_copy(d).wait_send()
    for u in range(USERS):
        out_ref[u : u + 1, :] = result[u]


def body(item_emb, confidences, user_block, item_block, block_age, block_count):
    dma = pltpu.SemaphoreType.DMA
    hbm = pl.BlockSpec(memory_space=pltpu.HBM)
    def hold(value):
        return pltpu.with_memory_space_constraint(value, pltpu.HBM)

    return pl.pallas_call(
        kernel,
        out_shape=jax.ShapeDtypeStruct((USERS, EMB), F32),
        in_specs=[hbm] * 6,
        out_specs=pl.BlockSpec(memory_space=pltpu.VMEM),
        scratch_shapes=[
            pltpu.VMEM((ROWS, EMB), F32),
            pltpu.VMEM((ROWS, EMB), BF16),
            pltpu.VMEM((STEPS, SLOTS), jnp.int32),
            pltpu.VMEM((STEPS, SLOTS), jnp.int32),
            pltpu.VMEM((STEPS, SLOTS), jnp.int32),
            pltpu.VMEM((1, STEPS), jnp.int32),
            pltpu.VMEM((Z, HELD, EMB), F32),
            pltpu.VMEM((Z, HELD, EMB), F32),
            pltpu.VMEM((HELD, EMB), F32),
            pltpu.VMEM((HELD, EMB), F32),
            pltpu.VMEM((STEPS, ROWS, EMB), F32),
            pltpu.VMEM((STEPS, EMB, ROWS), F32),
            pltpu.VMEM((STEPS, ROWS, 2 * EMB), BF16),
            pltpu.VMEM((SIDE, BLOCK, EMB), F32),
            pltpu.VMEM((SIDE, BLOCK, EMB), F32),
            pltpu.VMEM((Y, BLOCK, EMB), F32),
            pltpu.VMEM((SIDE, BLOCK, EMB), F32),
            pltpu.VMEM((USERS, 1, EMB), F32),
            dma((6,)), dma((Z,)), dma((Z,)), dma(()), dma(()),
            dma((3, CHUNKS)), dma((3, CHUNKS)),
            dma((SIDE,)), dma((SIDE,)), dma((Y,)), dma((Y,)), dma((SIDE,)), dma((SIDE,)),
            dma((Z,)), dma((Z,)),
        ],
        compiler_params=pltpu.CompilerParams(
            collective_id=0, has_side_effects=True, vmem_limit_bytes=32 << 20
        ),
        name="als_half_sweep",
    )(
        hold(item_emb),
        hold(confidences.reshape(ROWS, EMB)),
        hold(user_block.reshape(STEPS, SLOTS)),
        hold(item_block.reshape(STEPS, SLOTS)),
        hold(block_age.reshape(STEPS, SLOTS)),
        hold(block_count.reshape(1, STEPS)),
    )


def solution(mesh):
    placed = (
        P("item", None),
        P("item", "split", None, None, None, None),
        P("item", "split", None, None),
        P("item", "split", None, None),
        P("item", "split", None, None),
        P("item", "split", None),
    )
    return jax.shard_map(
        body, mesh=mesh, in_specs=placed, out_specs=P("item", None), check_vma=False
    )
```

```python
import jax
import jax.numpy as jnp
from jax import lax
from jax.experimental import pallas as pl
from jax.experimental.pallas import tpu as pltpu
from jax.sharding import PartitionSpec as P

CG_ITERS = 3
STEPS = 4
SLOTS = 16
USERS = 24
EMB = 128
ROWS = 512
X, Y, C = 4, 4, 2
N_ITEM = X * Y * C
Z = 12
NEAR = Y * C
BLOCK = EMB // NEAR
NEARBY = ((3, 0), (3, 1), (2, 0), (2, 1), (1, 0), (1, 1), (0, 1))
CHUNKS = 2
CHUNK = ROWS // CHUNKS
RIDGE = 0.1
HELD = 40
SENT = 33
FAR_FIRST = (6, 5, 7, 4, 8, 3, 9, 2, 10, 1, 11)
F32 = jnp.float32
BF16 = jnp.bfloat16
MESH = pl.DeviceIdType.MESH


def high_low(value):
    high = value.astype(BF16)
    return high, (value - high.astype(F32)).astype(BF16)


def block_weights(user_block, item_block, block_age, block_count):
    lane = lax.broadcasted_iota(jnp.int32, (STEPS, SLOTS), 1)
    row = lax.broadcasted_iota(jnp.int32, (STEPS, STEPS), 0)
    col = lax.broadcasted_iota(jnp.int32, (STEPS, STEPS), 1)
    counts = jnp.broadcast_to(block_count.astype(F32), (STEPS, STEPS))
    counts = jnp.sum(jnp.where(row == col, counts, 0.0), axis=1, keepdims=True)
    recency = 2.0 / (2.0 + block_age.astype(F32))
    recency = jnp.where(lane.astype(F32) < counts, recency, 0.0)
    code = (user_block * 4 + item_block).astype(F32)
    both = jnp.concatenate([recency, code], axis=0)
    slot = lax.broadcasted_iota(jnp.int32, (SLOTS, EMB), 0)
    spread = lax.broadcasted_iota(jnp.int32, (SLOTS, EMB), 1) // 8
    spread = jnp.where(slot == spread, 1.0, 0.0).astype(F32)
    return jnp.dot(both, spread, precision=lax.Precision.HIGHEST, preferred_element_type=F32)


def kernel(
    emb_hbm, conf_hbm, user_hbm, item_hbm, age_hbm, count_hbm, out_ref,
    emb_ref, conf_ref, user_ref, item_ref, age_ref, count_ref,
    send_a, recv_a, pair_a, recv_b,
    window, window_t, split_w, local_gram, gram_1, gram_2, gram_3, result,
    sem_in, sem_as, sem_ar, sem_bs, sem_br,
    sem_ws, sem_wr, sem_g1s, sem_g1r, sem_g2s, sem_g2r, sem_g3s, sem_g3r,
    sem_xs, sem_xr,
):
    item = lax.axis_index("item")
    split = lax.axis_index("split")
    core = lax.rem(item, C)
    near = lax.rem(item, NEAR)
    at_x = item // NEAR
    at_y = near // C
    y_hi = split // Z
    at_z = lax.rem(split, Z)
    partner = (1 - y_hi) * Z + at_z
    last_y = (at_y == Y - 1).astype(jnp.int32)
    first_y = (at_y == 0).astype(jnp.int32)
    next_split = (y_hi + last_y * (1 - 2 * y_hi)) * Z + at_z
    prev_split = (y_hi + first_y * (1 - 2 * y_hi)) * Z + at_z
    next_item = lax.rem(item + C, N_ITEM)
    prev_item = lax.rem(item + N_ITEM - C, N_ITEM)
    cross_next = lax.rem(item + 1, N_ITEM)
    cross_prev = lax.rem(item + N_ITEM - 1, N_ITEM)
    other_core = item + 1 - 2 * core

    def at_depth(d):
        return lax.rem(at_z + d, Z)

    def along_y(step, turn):
        place = lax.rem(y_hi * Y + at_y + step + 2 * Y, 2 * Y)
        peer = lax.rem(place, Y) * C + lax.rem(core + turn, C)
        return peer, (at_x * NEAR + peer, place // Y * Z + at_z)

    def along_x(d):
        peer = lax.rem(at_x + d, X)
        return peer, (peer * NEAR + near, split)

    barrier = pltpu.get_barrier_semaphore()

    def greet(device):
        pl.semaphore_signal(barrier, inc=1, device_id=device, device_id_type=MESH)

    for d in FAR_FIRST:
        greet((item, y_hi * Z + at_depth(d)))
    greet((item, partner))
    for step, turn in NEARBY:
        greet(along_y(-step, turn)[1])
        if step:
            greet(along_y(step, turn)[1])
    for d in range(1, X):
        greet(along_x(d)[1])
    greet((next_item, next_split))
    greet((prev_item, prev_split))

    @pl.when(core == 1)
    def _():
        greet((cross_next, next_split))

    @pl.when(core == 0)
    def _():
        greet((cross_prev, prev_split))

    loads = [
        pltpu.make_async_copy(src, dst, sem_in.at[n])
        for n, (src, dst) in enumerate(
            (
                (user_hbm, user_ref),
                (item_hbm, item_ref),
                (age_hbm, age_ref),
                (count_hbm, count_ref),
                (conf_hbm, conf_ref),
                (emb_hbm, emb_ref),
            )
        )
    ]
    for load in loads:
        load.start()

    def copy(src, dst, send_sem, recv_sem, device):
        return pltpu.make_async_remote_copy(
            src_ref=src, dst_ref=dst, send_sem=send_sem, recv_sem=recv_sem,
            device_id=device, device_id_type=MESH,
        )

    for load in loads[:4]:
        load.wait()
    spread = block_weights(user_ref[...], item_ref[...], age_ref[...], count_ref[...])
    half = USERS * 8
    row = lax.broadcasted_iota(jnp.int32, (half, 1), 0)
    row_user = row // 8
    row_code = ((row_user // 8) * 4 + lax.rem(row, 4)) * 16
    row_code = row_code + (lax.rem(row, 8) // 4) * 8 + lax.rem(row_user, 8)
    row_code = row_code.astype(F32)
    lane = lax.broadcasted_iota(jnp.int32, (1, 2 * EMB), 1)
    lane_code = (lane // EMB * 8 + lax.rem(lane, 8)).astype(F32)
    ones = jnp.ones((2 * EMB, EMB), BF16)
    rows_8 = lax.broadcasted_iota(jnp.int32, (8, EMB), 0)
    lanes_8 = lax.broadcasted_iota(jnp.int32, (8, EMB), 1)
    recency_rows = [jnp.zeros((1, EMB), F32) for _ in range(3)]
    loads[4].wait()
    for pair in range(2):
        k = 2 * pair
        recency = jnp.concatenate([spread[k : k + 1], spread[k + 1 : k + 2]], axis=1)
        code = jnp.concatenate([spread[4 + k : 5 + k], spread[5 + k : 6 + k]], axis=1)
        code = code * 16.0 + lane_code
        place = jnp.where(row_code == code, recency, 0.0)
        high, rest = high_low(place)
        low = (place - high.astype(F32) - rest.astype(F32)).astype(BF16)
        values = jnp.concatenate([conf_ref[pl.ds(2 * EMB * pair, 2 * EMB), :], ones], axis=1)
        sums = jnp.dot(
            jnp.concatenate([high, rest, low], axis=0), values, preferred_element_type=F32
        )
        sums = sums[:half] + sums[half : 2 * half] + sums[2 * half :]
        by_user = sums[:, :EMB].reshape(Z, 2, 8, EMB)
        for u in range(2):
            send_a[:, pl.ds(SLOTS * u + 8 * pair, 8), :] = by_user[:, u]
        for block in range(3):
            part = sums[64 * block : 64 * block + 8, EMB:]
            part = jnp.where(lanes_8 == rows_8 + 8 * pair, part, 0.0)
            recency_rows[block] = recency_rows[block] + jnp.sum(part, axis=0, keepdims=True)
    for peer in range(Z):
        send_a[peer, 2 * SLOTS : 2 * SLOTS + 1, :] = recency_rows[peer // 4]

    def prepare(slot, rows):
        high, low = high_low(rows)
        split_w[slot, :, pl.ds(0, EMB)] = high
        split_w[slot, :, pl.ds(EMB, EMB)] = low
        turned = rows.T
        window_t[slot] = turned
        return turned

    def three_products(left, slot):
        high, low = high_low(left)
        count = left.shape[0]
        both = jnp.concatenate([high, low], axis=0)
        out = jnp.dot(both, split_w[slot], preferred_element_type=F32)
        return out[:count, :EMB] + out[:count, EMB:] + out[count:, :EMB]

    loads[5].wait()
    turned = prepare(0, emb_ref[...])
    local_gram[...] = three_products(turned, 0).reshape(NEAR, BLOCK, EMB)

    pl.semaphore_wait(barrier, Z - 1 + 1 + 13 + X - 1 + 3)

    def chunk(c):
        return pl.ds(c * CHUNK, CHUNK)

    def own_next(c):
        return copy(
            emb_ref.at[chunk(c)], window.at[2, chunk(c)],
            sem_ws.at[0, c], sem_wr.at[1, c], (next_item, next_split),
        )

    def own_core(c):
        return copy(
            emb_ref.at[chunk(c)], window.at[1, chunk(c)],
            sem_ws.at[1, c], sem_wr.at[0, c], (other_core, split),
        )

    def relay_core(c, slot, send_slot):
        return copy(
            window.at[2, chunk(c)], window.at[slot, chunk(c)],
            sem_ws.at[send_slot, c], sem_wr.at[slot - 1, c], (other_core, split),
        )

    def relay_next(c):
        return copy(
            window.at[2, chunk(c)], window.at[3, chunk(c)],
            sem_ws.at[2, c], sem_wr.at[2, c], (cross_next, next_split),
        )

    def pass_on(c):
        own_next(c).wait_recv()

        @pl.when(core == 1)
        def _():
            relay_next(c).start()

    def share(c):
        @pl.when(core == 0)
        def _():
            relay_core(c, 3, 2).start()

        @pl.when(core == 1)
        def _():
            relay_core(c, 1, 1).start()

    def depth_copy(d):
        peer = at_depth(d)
        return copy(
            send_a.at[peer, pl.ds(0, SENT)], recv_a.at[at_z, pl.ds(0, SENT)],
            sem_as.at[d], sem_ar.at[at_z], (item, y_hi * Z + peer),
        )

    def gram_copy_1(n):
        peer, device = along_y(-NEARBY[n][0], NEARBY[n][1])
        return copy(
            local_gram.at[peer], gram_1.at[near], sem_g1s.at[n], sem_g1r.at[near], device
        )

    def gram_copy_2(d):
        return copy(
            gram_2.at[at_x], gram_2.at[at_x], sem_g2s.at[d], sem_g2r.at[at_x], along_x(d)[1]
        )

    def gram_copy_3(n):
        device = along_y(-NEARBY[n][0], NEARBY[n][1])[1]
        return copy(
            gram_3.at[near], gram_3.at[near], sem_g3s.at[n], sem_g3r.at[near], device
        )

    for d in FAR_FIRST:
        depth_copy(d).start()
    for n in range(NEAR - 1):
        gram_copy_1(n).start()
    for c in range(CHUNKS):
        own_next(c).start()

    @pl.when(core == 0)
    def _():
        for c in range(CHUNKS):
            own_core(c).start()

    total = local_gram[near]
    for n, (step, turn) in enumerate(NEARBY):
        peer, device = along_y(step, turn)
        copy(
            local_gram.at[peer], gram_1.at[peer], sem_g1s.at[n], sem_g1r.at[peer], device
        ).wait_recv()
        total = total + gram_1[peer]
    gram_2[at_x] = total
    for d in range(1, X):
        gram_copy_2(d).start()

    pass_on(0)

    for c in range(1, CHUNKS):
        pass_on(c)

    def sum_z(d, total):
        peer = at_depth(d)
        copy(
            send_a.at[0, pl.ds(0, SENT)], recv_a.at[peer, pl.ds(0, SENT)],
            sem_as.at[d], sem_ar.at[peer], (item, y_hi * Z + peer),
        ).wait_recv()
        return total + recv_a[peer, pl.ds(0, SENT)]

    pair_a[pl.ds(0, SENT)] = lax.fori_loop(1, Z, sum_z, send_a[at_z, pl.ds(0, SENT)])
    send_pair = copy(
        pair_a.at[pl.ds(0, SENT)], recv_b.at[pl.ds(0, SENT)], sem_bs, sem_br, (item, partner)
    )
    send_pair.start()

    for c in range(CHUNKS):
        share(c)

    for d in range(1, X):
        peer, device = along_x(d)
        copy(
            gram_2.at[peer], gram_2.at[peer], sem_g2s.at[d], sem_g2r.at[peer], device
        ).wait_recv()
    gram_3[near] = gram_2[0] + gram_2[1] + gram_2[2] + gram_2[3]
    for n in range(NEAR - 1):
        gram_copy_3(n).start()

    prepare(2, window[2])
    for slot in (1, 3):
        for c in range(CHUNKS):
            copy(
                window.at[2, chunk(c)], window.at[slot, chunk(c)],
                sem_ws.at[0, c], sem_wr.at[slot - 1, c], (other_core, split),
            ).wait_recv()
        prepare(slot, window[slot])
    for n, (step, turn) in enumerate(NEARBY):
        peer, device = along_y(step, turn)
        copy(
            gram_3.at[peer], gram_3.at[peer], sem_g3s.at[n], sem_g3r.at[peer], device
        ).wait_recv()
    eye = lax.broadcasted_iota(jnp.int32, (EMB, EMB), 0)
    eye = eye == lax.broadcasted_iota(jnp.int32, (EMB, EMB), 1)
    base = gram_3[...].reshape(EMB, EMB) + jnp.where(eye, RIDGE, 0.0)

    send_pair.wait_recv()
    both = pair_a[pl.ds(0, SENT)] + recv_b[pl.ds(0, SENT)]
    weights = both[: 2 * SLOTS].reshape(2, SLOTS, EMB)
    block_row = jnp.broadcast_to(both[2 * SLOTS : 2 * SLOTS + 1], (SLOTS, EMB))
    rows_16 = lax.broadcasted_iota(jnp.int32, (SLOTS, EMB), 0)
    lanes_16 = lax.broadcasted_iota(jnp.int32, (SLOTS, EMB), 1)
    block_col = jnp.sum(jnp.where(rows_16 == lanes_16, block_row, 0.0), axis=1, keepdims=True)

    def weighted(slot):
        base_row = 4 * slot
        parts = []
        for u in range(2):
            wishes = weights[u] + block_col
            parts.append(
                jnp.concatenate(
                    [
                        window_t[slot, :, pl.ds(b * EMB, EMB)]
                        * weights[u, base_row + b : base_row + b + 1]
                        for b in range(4)
                    ],
                    axis=1,
                )
            )
            wish = jnp.concatenate(
                [wishes[base_row + b : base_row + b + 1] for b in range(4)], axis=1
            )
            parts.append(jnp.broadcast_to(wish, (8, ROWS)))
        return three_products(jnp.concatenate(parts, axis=0), slot)

    system = weighted(0)
    for slot in range(1, STEPS):
        system = system + weighted(slot)

    def over(value):
        return jnp.sum(value, axis=1, keepdims=True)

    stride = EMB + 8
    matrices = [system[u * stride : u * stride + EMB] + base for u in range(2)]
    right = jnp.concatenate(
        [system[u * stride + EMB : (u + 1) * stride] for u in range(2)], axis=0
    )
    answer = jnp.zeros_like(right)
    residual = right
    direction = right
    norm_now = over(residual * residual)
    for _ in range(CG_ITERS):
        image = jnp.concatenate(
            [
                jnp.dot(
                    direction[8 * u : 8 * u + 8], matrices[u],
                    precision=lax.Precision.HIGHEST, preferred_element_type=F32,
                )
                for u in range(2)
            ],
            axis=0,
        )
        step_size = norm_now / over(direction * image)
        answer = answer + step_size * direction
        residual = residual - step_size * image
        norm_next = over(residual * residual)
        direction = residual + (norm_next / norm_now) * direction
        norm_now = norm_next
    result[2 * at_z] = answer[:1]
    result[2 * at_z + 1] = answer[8:9]

    def answer_copy(d):
        return copy(
            result.at[pl.ds(2 * at_z, 2)], result.at[pl.ds(2 * at_z, 2)],
            sem_xs.at[d], sem_xr.at[at_z], (item, y_hi * Z + at_depth(d)),
        )

    for d in FAR_FIRST:
        answer_copy(d).start()

    for c in range(CHUNKS):
        own_next(c).wait_send()
        relay_core(c, 1, 1).wait_send()
        relay_next(c).wait_send()
    for d in range(1, Z):
        depth_copy(d).wait_send()
    send_pair.wait_send()
    for n in range(NEAR - 1):
        gram_copy_1(n).wait_send()
        gram_copy_3(n).wait_send()
    for d in range(1, X):
        gram_copy_2(d).wait_send()
    for d in range(1, Z):
        peer = at_depth(d)
        copy(
            result.at[pl.ds(2 * peer, 2)], result.at[pl.ds(2 * peer, 2)],
            sem_xs.at[d], sem_xr.at[peer], (item, y_hi * Z + peer),
        ).wait_recv()
    for d in range(1, Z):
        answer_copy(d).wait_send()
    for u in range(USERS):
        out_ref[u : u + 1, :] = result[u]


def body(item_emb, confidences, user_block, item_block, block_age, block_count):
    dma = pltpu.SemaphoreType.DMA
    hbm = pl.BlockSpec(memory_space=pltpu.HBM)
    def hold(value):
        return pltpu.with_memory_space_constraint(value, pltpu.HBM)

    return pl.pallas_call(
        kernel,
        out_shape=jax.ShapeDtypeStruct((USERS, EMB), F32),
        in_specs=[hbm] * 6,
        out_specs=pl.BlockSpec(memory_space=pltpu.VMEM),
        scratch_shapes=[
            pltpu.VMEM((ROWS, EMB), F32),
            pltpu.VMEM((ROWS, EMB), BF16),
            pltpu.VMEM((STEPS, SLOTS), jnp.int32),
            pltpu.VMEM((STEPS, SLOTS), jnp.int32),
            pltpu.VMEM((STEPS, SLOTS), jnp.int32),
            pltpu.VMEM((1, STEPS), jnp.int32),
            pltpu.VMEM((Z, HELD, EMB), F32),
            pltpu.VMEM((Z, HELD, EMB), F32),
            pltpu.VMEM((HELD, EMB), F32),
            pltpu.VMEM((HELD, EMB), F32),
            pltpu.VMEM((STEPS, ROWS, EMB), F32),
            pltpu.VMEM((STEPS, EMB, ROWS), F32),
            pltpu.VMEM((STEPS, ROWS, 2 * EMB), BF16),
            pltpu.VMEM((NEAR, BLOCK, EMB), F32),
            pltpu.VMEM((NEAR, BLOCK, EMB), F32),
            pltpu.VMEM((X, BLOCK, EMB), F32),
            pltpu.VMEM((NEAR, BLOCK, EMB), F32),
            pltpu.VMEM((USERS, 1, EMB), F32),
            dma((6,)), dma((Z,)), dma((Z,)), dma(()), dma(()),
            dma((3, CHUNKS)), dma((3, CHUNKS)),
            dma((NEAR,)), dma((NEAR,)), dma((X,)), dma((X,)), dma((NEAR,)), dma((NEAR,)),
            dma((Z,)), dma((Z,)),
        ],
        compiler_params=pltpu.CompilerParams(
            collective_id=0, has_side_effects=True, vmem_limit_bytes=32 << 20
        ),
        name="als_half_sweep",
    )(
        hold(item_emb),
        hold(confidences.reshape(ROWS, EMB)),
        hold(user_block.reshape(STEPS, SLOTS)),
        hold(item_block.reshape(STEPS, SLOTS)),
        hold(block_age.reshape(STEPS, SLOTS)),
        hold(block_count.reshape(1, STEPS)),
    )


def solution(mesh):
    placed = (
        P("item", None),
        P("item", "split", None, None, None, None),
        P("item", "split", None, None),
        P("item", "split", None, None),
        P("item", "split", None, None),
        P("item", "split", None),
    )
    return jax.shard_map(
        body, mesh=mesh, in_specs=placed, out_specs=P("item", None), check_vma=False
    )
```

```python
import jax
import jax.numpy as jnp
from jax import lax
from jax.experimental import pallas as pl
from jax.experimental.pallas import tpu as pltpu
from jax.sharding import PartitionSpec as P

CG_ITERS = 3
STEPS = 4
SLOTS = 16
USERS = 24
EMB = 128
ROWS = 512
X, Y, C = 4, 4, 2
N_ITEM = X * Y * C
Z = 12
NEAR = Y * C
OWNERS = 2 * C
BLOCK = EMB // OWNERS
NEARBY = ((3, 0), (3, 1), (2, 0), (2, 1), (1, 0), (1, 1), (0, 1))
CHUNKS = 2
CHUNK = ROWS // CHUNKS
RIDGE = 0.1
HELD = 40
SENT = 33
FAR_FIRST = (6, 5, 7, 4, 8, 3, 9, 2, 10, 1, 11)
F32 = jnp.float32
BF16 = jnp.bfloat16
MESH = pl.DeviceIdType.MESH


def high_low(value):
    high = value.astype(BF16)
    return high, (value - high.astype(F32)).astype(BF16)


def block_weights(user_block, item_block, block_age, block_count):
    lane = lax.broadcasted_iota(jnp.int32, (STEPS, SLOTS), 1)
    row = lax.broadcasted_iota(jnp.int32, (STEPS, STEPS), 0)
    col = lax.broadcasted_iota(jnp.int32, (STEPS, STEPS), 1)
    counts = jnp.broadcast_to(block_count.astype(F32), (STEPS, STEPS))
    counts = jnp.sum(jnp.where(row == col, counts, 0.0), axis=1, keepdims=True)
    recency = 2.0 / (2.0 + block_age.astype(F32))
    recency = jnp.where(lane.astype(F32) < counts, recency, 0.0)
    code = (user_block * 4 + item_block).astype(F32)
    both = jnp.concatenate([recency, code], axis=0)
    slot = lax.broadcasted_iota(jnp.int32, (SLOTS, EMB), 0)
    spread = lax.broadcasted_iota(jnp.int32, (SLOTS, EMB), 1) // 8
    spread = jnp.where(slot == spread, 1.0, 0.0).astype(F32)
    return jnp.dot(both, spread, precision=lax.Precision.HIGHEST, preferred_element_type=F32)


def kernel(
    emb_hbm, conf_hbm, user_hbm, item_hbm, age_hbm, count_hbm, out_ref,
    emb_ref, conf_ref, user_ref, item_ref, age_ref, count_ref,
    send_a, recv_a, pair_a, recv_b,
    window, window_t, split_w, local_gram, gram_1, gram_2, gram_3, result,
    sem_in, sem_as, sem_ar, sem_bs, sem_br,
    sem_ws, sem_wr, sem_g1s, sem_g1r, sem_g2s, sem_g2r, sem_g3s, sem_g3r,
    sem_xs, sem_xr,
):
    item = lax.axis_index("item")
    split = lax.axis_index("split")
    core = lax.rem(item, C)
    near = lax.rem(item, NEAR)
    at_x = item // NEAR
    at_y = near // C
    y_hi = split // Z
    at_z = lax.rem(split, Z)
    partner = (1 - y_hi) * Z + at_z
    last_y = (at_y == Y - 1).astype(jnp.int32)
    first_y = (at_y == 0).astype(jnp.int32)
    next_split = (y_hi + last_y * (1 - 2 * y_hi)) * Z + at_z
    prev_split = (y_hi + first_y * (1 - 2 * y_hi)) * Z + at_z
    next_item = lax.rem(item + C, N_ITEM)
    prev_item = lax.rem(item + N_ITEM - C, N_ITEM)
    cross_next = lax.rem(item + 1, N_ITEM)
    cross_prev = lax.rem(item + N_ITEM - 1, N_ITEM)
    other_core = item + 1 - 2 * core

    def at_depth(d):
        return lax.rem(at_z + d, Z)

    def along_y(step, turn):
        place = lax.rem(y_hi * Y + at_y + step + 2 * Y, 2 * Y)
        peer = lax.rem(place, Y) * C + lax.rem(core + turn, C)
        return peer, (at_x * NEAR + peer, place // Y * Z + at_z)

    owner = near - C
    owns = jnp.logical_and(at_y >= 1, at_y <= 2)

    def owner_at(n, sign):
        step = lax.rem(sign * (1 + n // C - at_y) + 2 * Y, Y)
        place = lax.rem(y_hi * Y + at_y + sign * step + 2 * Y, 2 * Y)
        return at_x * NEAR + (1 + n // C) * C + n % C, place // Y * Z + at_z

    def along_x(d):
        peer = lax.rem(at_x + d, X)
        return peer, (peer * NEAR + near, split)

    barrier = pltpu.get_barrier_semaphore()

    def greet(device):
        pl.semaphore_signal(barrier, inc=1, device_id=device, device_id_type=MESH)

    for d in FAR_FIRST:
        greet((item, y_hi * Z + at_depth(d)))
    greet((item, partner))
    for step, turn in NEARBY:
        greet(along_y(-step, turn)[1])
        if step:
            greet(along_y(step, turn)[1])
    for d in range(1, X):
        greet(along_x(d)[1])
    greet((next_item, next_split))
    greet((prev_item, prev_split))

    @pl.when(core == 1)
    def _():
        greet((cross_next, next_split))

    @pl.when(core == 0)
    def _():
        greet((cross_prev, prev_split))

    loads = [
        pltpu.make_async_copy(src, dst, sem_in.at[n])
        for n, (src, dst) in enumerate(
            (
                (user_hbm, user_ref),
                (item_hbm, item_ref),
                (age_hbm, age_ref),
                (count_hbm, count_ref),
                (conf_hbm, conf_ref),
                (emb_hbm, emb_ref),
            )
        )
    ]
    for load in loads:
        load.start()

    def copy(src, dst, send_sem, recv_sem, device):
        return pltpu.make_async_remote_copy(
            src_ref=src, dst_ref=dst, send_sem=send_sem, recv_sem=recv_sem,
            device_id=device, device_id_type=MESH,
        )

    for load in loads[:4]:
        load.wait()
    spread = block_weights(user_ref[...], item_ref[...], age_ref[...], count_ref[...])
    half = USERS * 8
    row = lax.broadcasted_iota(jnp.int32, (half, 1), 0)
    row_user = row // 8
    row_code = ((row_user // 8) * 4 + lax.rem(row, 4)) * 16
    row_code = row_code + (lax.rem(row, 8) // 4) * 8 + lax.rem(row_user, 8)
    row_code = row_code.astype(F32)
    lane = lax.broadcasted_iota(jnp.int32, (1, 2 * EMB), 1)
    lane_code = (lane // EMB * 8 + lax.rem(lane, 8)).astype(F32)
    ones = jnp.ones((2 * EMB, EMB), BF16)
    rows_8 = lax.broadcasted_iota(jnp.int32, (8, EMB), 0)
    lanes_8 = lax.broadcasted_iota(jnp.int32, (8, EMB), 1)
    recency_rows = [jnp.zeros((1, EMB), F32) for _ in range(3)]
    loads[4].wait()
    for pair in range(2):
        k = 2 * pair
        recency = jnp.concatenate([spread[k : k + 1], spread[k + 1 : k + 2]], axis=1)
        code = jnp.concatenate([spread[4 + k : 5 + k], spread[5 + k : 6 + k]], axis=1)
        code = code * 16.0 + lane_code
        place = jnp.where(row_code == code, recency, 0.0)
        high, rest = high_low(place)
        low = (place - high.astype(F32) - rest.astype(F32)).astype(BF16)
        values = jnp.concatenate([conf_ref[pl.ds(2 * EMB * pair, 2 * EMB), :], ones], axis=1)
        sums = jnp.dot(
            jnp.concatenate([high, rest, low], axis=0), values, preferred_element_type=F32
        )
        sums = sums[:half] + sums[half : 2 * half] + sums[2 * half :]
        by_user = sums[:, :EMB].reshape(Z, 2, 8, EMB)
        for u in range(2):
            send_a[:, pl.ds(SLOTS * u + 8 * pair, 8), :] = by_user[:, u]
        for block in range(3):
            part = sums[64 * block : 64 * block + 8, EMB:]
            part = jnp.where(lanes_8 == rows_8 + 8 * pair, part, 0.0)
            recency_rows[block] = recency_rows[block] + jnp.sum(part, axis=0, keepdims=True)
    for peer in range(Z):
        send_a[peer, 2 * SLOTS : 2 * SLOTS + 1, :] = recency_rows[peer // 4]

    def prepare(slot, rows):
        high, low = high_low(rows)
        split_w[slot, :, pl.ds(0, EMB)] = high
        split_w[slot, :, pl.ds(EMB, EMB)] = low
        turned = rows.T
        window_t[slot] = turned
        return turned

    def three_products(left, slot):
        high, low = high_low(left)
        count = left.shape[0]
        both = jnp.concatenate([high, low], axis=0)
        out = jnp.dot(both, split_w[slot], preferred_element_type=F32)
        return out[:count, :EMB] + out[:count, EMB:] + out[count:, :EMB]

    loads[5].wait()
    turned = prepare(0, emb_ref[...])
    local_gram[...] = three_products(turned, 0).reshape(OWNERS, BLOCK, EMB)

    pl.semaphore_wait(barrier, Z - 1 + 1 + 13 + X - 1 + 3)

    def chunk(c):
        return pl.ds(c * CHUNK, CHUNK)

    def own_next(c):
        return copy(
            emb_ref.at[chunk(c)], window.at[2, chunk(c)],
            sem_ws.at[0, c], sem_wr.at[1, c], (next_item, next_split),
        )

    def own_core(c):
        return copy(
            emb_ref.at[chunk(c)], window.at[1, chunk(c)],
            sem_ws.at[1, c], sem_wr.at[0, c], (other_core, split),
        )

    def relay_core(c, slot, send_slot):
        return copy(
            window.at[2, chunk(c)], window.at[slot, chunk(c)],
            sem_ws.at[send_slot, c], sem_wr.at[slot - 1, c], (other_core, split),
        )

    def relay_next(c):
        return copy(
            window.at[2, chunk(c)], window.at[3, chunk(c)],
            sem_ws.at[2, c], sem_wr.at[2, c], (cross_next, next_split),
        )

    def pass_on(c):
        own_next(c).wait_recv()

        @pl.when(core == 1)
        def _():
            relay_next(c).start()

    def share(c):
        @pl.when(core == 0)
        def _():
            relay_core(c, 3, 2).start()

        @pl.when(core == 1)
        def _():
            relay_core(c, 1, 1).start()

    def depth_copy(d):
        peer = at_depth(d)
        return copy(
            send_a.at[peer, pl.ds(0, SENT)], recv_a.at[at_z, pl.ds(0, SENT)],
            sem_as.at[d], sem_ar.at[at_z], (item, y_hi * Z + peer),
        )

    def gram_copy_1(n):
        return copy(
            local_gram.at[n], gram_1.at[near], sem_g1s.at[n], sem_g1r.at[near], owner_at(n, -1)
        )

    def gram_copy_2(d):
        return copy(
            gram_2.at[at_x], gram_2.at[at_x], sem_g2s.at[d], sem_g2r.at[at_x], along_x(d)[1]
        )

    def gram_copy_3(n):
        device = along_y(-NEARBY[n][0], NEARBY[n][1])[1]
        return copy(
            gram_3.at[owner], gram_3.at[owner], sem_g3s.at[n], sem_g3r.at[owner], device
        )

    def for_other_owners(act):
        for n in range(OWNERS):

            @pl.when(owner != n)
            def _():
                act(n)

    for d in FAR_FIRST:
        depth_copy(d).start()
    for_other_owners(lambda n: gram_copy_1(n).start())
    for c in range(CHUNKS):
        own_next(c).start()

    @pl.when(core == 0)
    def _():
        for c in range(CHUNKS):
            own_core(c).start()

    @pl.when(owns)
    def _():
        total = local_gram[owner]
        for step, turn in NEARBY:
            peer, device = along_y(step, turn)
            copy(
                local_gram.at[0], gram_1.at[peer], sem_g1s.at[0], sem_g1r.at[peer], device
            ).wait_recv()
            total = total + gram_1[peer]
        gram_2[at_x] = total
        for d in range(1, X):
            gram_copy_2(d).start()

    pass_on(0)

    for c in range(1, CHUNKS):
        pass_on(c)

    def sum_z(d, total):
        peer = at_depth(d)
        copy(
            send_a.at[0, pl.ds(0, SENT)], recv_a.at[peer, pl.ds(0, SENT)],
            sem_as.at[d], sem_ar.at[peer], (item, y_hi * Z + peer),
        ).wait_recv()
        return total + recv_a[peer, pl.ds(0, SENT)]

    pair_a[pl.ds(0, SENT)] = lax.fori_loop(1, Z, sum_z, send_a[at_z, pl.ds(0, SENT)])
    send_pair = copy(
        pair_a.at[pl.ds(0, SENT)], recv_b.at[pl.ds(0, SENT)], sem_bs, sem_br, (item, partner)
    )
    send_pair.start()

    for c in range(CHUNKS):
        share(c)

    @pl.when(owns)
    def _():
        for d in range(1, X):
            peer, device = along_x(d)
            copy(
                gram_2.at[peer], gram_2.at[peer], sem_g2s.at[d], sem_g2r.at[peer], device
            ).wait_recv()
        gram_3[owner] = gram_2[0] + gram_2[1] + gram_2[2] + gram_2[3]
        for n in range(NEAR - 1):
            gram_copy_3(n).start()

    prepare(2, window[2])
    for slot in (1, 3):
        for c in range(CHUNKS):
            copy(
                window.at[2, chunk(c)], window.at[slot, chunk(c)],
                sem_ws.at[0, c], sem_wr.at[slot - 1, c], (other_core, split),
            ).wait_recv()
        prepare(slot, window[slot])
    for_other_owners(
        lambda n: copy(
            gram_3.at[n], gram_3.at[n], sem_g3s.at[0], sem_g3r.at[n], owner_at(n, 1)
        ).wait_recv()
    )
    eye = lax.broadcasted_iota(jnp.int32, (EMB, EMB), 0)
    eye = eye == lax.broadcasted_iota(jnp.int32, (EMB, EMB), 1)
    base = gram_3[...].reshape(EMB, EMB) + jnp.where(eye, RIDGE, 0.0)

    send_pair.wait_recv()
    both = pair_a[pl.ds(0, SENT)] + recv_b[pl.ds(0, SENT)]
    weights = both[: 2 * SLOTS].reshape(2, SLOTS, EMB)
    block_row = jnp.broadcast_to(both[2 * SLOTS : 2 * SLOTS + 1], (SLOTS, EMB))
    rows_16 = lax.broadcasted_iota(jnp.int32, (SLOTS, EMB), 0)
    lanes_16 = lax.broadcasted_iota(jnp.int32, (SLOTS, EMB), 1)
    block_col = jnp.sum(jnp.where(rows_16 == lanes_16, block_row, 0.0), axis=1, keepdims=True)

    def weighted(slot):
        base_row = 4 * slot
        parts = []
        for u in range(2):
            wishes = weights[u] + block_col
            parts.append(
                jnp.concatenate(
                    [
                        window_t[slot, :, pl.ds(b * EMB, EMB)]
                        * weights[u, base_row + b : base_row + b + 1]
                        for b in range(4)
                    ],
                    axis=1,
                )
            )
            wish = jnp.concatenate(
                [wishes[base_row + b : base_row + b + 1] for b in range(4)], axis=1
            )
            parts.append(jnp.broadcast_to(wish, (8, ROWS)))
        return three_products(jnp.concatenate(parts, axis=0), slot)

    system = weighted(0)
    for slot in range(1, STEPS):
        system = system + weighted(slot)

    def over(value):
        return jnp.sum(value, axis=1, keepdims=True)

    stride = EMB + 8
    matrices = [system[u * stride : u * stride + EMB] + base for u in range(2)]
    right = jnp.concatenate(
        [system[u * stride + EMB : (u + 1) * stride] for u in range(2)], axis=0
    )
    answer = jnp.zeros_like(right)
    residual = right
    direction = right
    norm_now = over(residual * residual)
    for _ in range(CG_ITERS):
        image = jnp.concatenate(
            [
                jnp.dot(
                    direction[8 * u : 8 * u + 8], matrices[u],
                    precision=lax.Precision.HIGHEST, preferred_element_type=F32,
                )
                for u in range(2)
            ],
            axis=0,
        )
        step_size = norm_now / over(direction * image)
        answer = answer + step_size * direction
        residual = residual - step_size * image
        norm_next = over(residual * residual)
        direction = residual + (norm_next / norm_now) * direction
        norm_now = norm_next
    result[2 * at_z] = answer[:1]
    result[2 * at_z + 1] = answer[8:9]

    def answer_copy(d):
        return copy(
            result.at[pl.ds(2 * at_z, 2)], result.at[pl.ds(2 * at_z, 2)],
            sem_xs.at[d], sem_xr.at[at_z], (item, y_hi * Z + at_depth(d)),
        )

    for d in FAR_FIRST:
        answer_copy(d).start()

    for c in range(CHUNKS):
        own_next(c).wait_send()
        relay_core(c, 1, 1).wait_send()
        relay_next(c).wait_send()
    for d in range(1, Z):
        depth_copy(d).wait_send()
    send_pair.wait_send()
    for_other_owners(lambda n: gram_copy_1(n).wait_send())

    @pl.when(owns)
    def _():
        for n in range(NEAR - 1):
            gram_copy_3(n).wait_send()
        for d in range(1, X):
            gram_copy_2(d).wait_send()

    for d in range(1, Z):
        peer = at_depth(d)
        copy(
            result.at[pl.ds(2 * peer, 2)], result.at[pl.ds(2 * peer, 2)],
            sem_xs.at[d], sem_xr.at[peer], (item, y_hi * Z + peer),
        ).wait_recv()
    for d in range(1, Z):
        answer_copy(d).wait_send()
    for u in range(USERS):
        out_ref[u : u + 1, :] = result[u]


def body(item_emb, confidences, user_block, item_block, block_age, block_count):
    dma = pltpu.SemaphoreType.DMA
    hbm = pl.BlockSpec(memory_space=pltpu.HBM)
    def hold(value):
        return pltpu.with_memory_space_constraint(value, pltpu.HBM)

    return pl.pallas_call(
        kernel,
        out_shape=jax.ShapeDtypeStruct((USERS, EMB), F32),
        in_specs=[hbm] * 6,
        out_specs=pl.BlockSpec(memory_space=pltpu.VMEM),
        scratch_shapes=[
            pltpu.VMEM((ROWS, EMB), F32),
            pltpu.VMEM((ROWS, EMB), BF16),
            pltpu.VMEM((STEPS, SLOTS), jnp.int32),
            pltpu.VMEM((STEPS, SLOTS), jnp.int32),
            pltpu.VMEM((STEPS, SLOTS), jnp.int32),
            pltpu.VMEM((1, STEPS), jnp.int32),
            pltpu.VMEM((Z, HELD, EMB), F32),
            pltpu.VMEM((Z, HELD, EMB), F32),
            pltpu.VMEM((HELD, EMB), F32),
            pltpu.VMEM((HELD, EMB), F32),
            pltpu.VMEM((STEPS, ROWS, EMB), F32),
            pltpu.VMEM((STEPS, EMB, ROWS), F32),
            pltpu.VMEM((STEPS, ROWS, 2 * EMB), BF16),
            pltpu.VMEM((OWNERS, BLOCK, EMB), F32),
            pltpu.VMEM((NEAR, BLOCK, EMB), F32),
            pltpu.VMEM((X, BLOCK, EMB), F32),
            pltpu.VMEM((OWNERS, BLOCK, EMB), F32),
            pltpu.VMEM((USERS, 1, EMB), F32),
            dma((6,)), dma((Z,)), dma((Z,)), dma(()), dma(()),
            dma((3, CHUNKS)), dma((3, CHUNKS)),
            dma((OWNERS,)), dma((NEAR,)), dma((X,)), dma((X,)), dma((NEAR,)), dma((OWNERS,)),
            dma((Z,)), dma((Z,)),
        ],
        compiler_params=pltpu.CompilerParams(
            collective_id=0, has_side_effects=True, vmem_limit_bytes=32 << 20
        ),
        name="als_half_sweep",
    )(
        hold(item_emb),
        hold(confidences.reshape(ROWS, EMB)),
        hold(user_block.reshape(STEPS, SLOTS)),
        hold(item_block.reshape(STEPS, SLOTS)),
        hold(block_age.reshape(STEPS, SLOTS)),
        hold(block_count.reshape(1, STEPS)),
    )


def solution(mesh):
    placed = (
        P("item", None),
        P("item", "split", None, None, None, None),
        P("item", "split", None, None),
        P("item", "split", None, None),
        P("item", "split", None, None),
        P("item", "split", None),
    )
    return jax.shard_map(
        body, mesh=mesh, in_specs=placed, out_specs=P("item", None), check_vma=False
    )
```

```python
import jax
import jax.numpy as jnp
from jax import lax
from jax.experimental import pallas as pl
from jax.experimental.pallas import tpu as pltpu
from jax.sharding import PartitionSpec as P

CG_ITERS = 3
STEPS = 4
SLOTS = 16
USERS = 24
EMB = 128
ROWS = 512
X, Y, C = 4, 4, 2
N_ITEM = X * Y * C
Z = 12
NEAR = Y * C
OWNERS = 2 * C
BLOCK = EMB // OWNERS
NEARBY = ((3, 0), (3, 1), (2, 0), (2, 1), (1, 0), (1, 1), (0, 1))
CHUNKS = 2
CHUNK = ROWS // CHUNKS
RIDGE = 0.1
HELD = 40
SENT = 33
FAR_FIRST = (6, 5, 7, 4, 8, 3, 9, 2, 10, 1, 11)
F32 = jnp.float32
BF16 = jnp.bfloat16
MESH = pl.DeviceIdType.MESH


def high_low(value):
    high = value.astype(BF16)
    return high, (value - high.astype(F32)).astype(BF16)


def block_weights(user_block, item_block, block_age, block_count):
    lane = lax.broadcasted_iota(jnp.int32, (STEPS, SLOTS), 1)
    row = lax.broadcasted_iota(jnp.int32, (STEPS, STEPS), 0)
    col = lax.broadcasted_iota(jnp.int32, (STEPS, STEPS), 1)
    counts = jnp.broadcast_to(block_count.astype(F32), (STEPS, STEPS))
    counts = jnp.sum(jnp.where(row == col, counts, 0.0), axis=1, keepdims=True)
    recency = 2.0 / (2.0 + block_age.astype(F32))
    recency = jnp.where(lane.astype(F32) < counts, recency, 0.0)
    code = (user_block * 4 + item_block).astype(F32)
    both = jnp.concatenate([recency, code], axis=0)
    slot = lax.broadcasted_iota(jnp.int32, (SLOTS, EMB), 0)
    spread = lax.broadcasted_iota(jnp.int32, (SLOTS, EMB), 1) // 8
    spread = jnp.where(slot == spread, 1.0, 0.0).astype(F32)
    return jnp.dot(both, spread, precision=lax.Precision.HIGHEST, preferred_element_type=F32)


def kernel(
    emb_hbm, conf_hbm, user_hbm, item_hbm, age_hbm, count_hbm, out_ref,
    emb_ref, conf_ref, user_ref, item_ref, age_ref, count_ref,
    send_a, recv_a, pair_a, recv_b,
    window, window_t, split_w, local_gram, gram_1, gram_2, gram_3, result,
    sem_in, sem_as, sem_ar, sem_bs, sem_br,
    sem_ws, sem_wr, sem_g1s, sem_g1r, sem_g2s, sem_g2r, sem_g3s, sem_g3r,
    sem_xs, sem_xr,
):
    item = lax.axis_index("item")
    split = lax.axis_index("split")
    core = lax.rem(item, C)
    near = lax.rem(item, NEAR)
    at_x = item // NEAR
    at_y = near // C
    y_hi = split // Z
    at_z = lax.rem(split, Z)
    partner = (1 - y_hi) * Z + at_z
    last_y = (at_y == Y - 1).astype(jnp.int32)
    first_y = (at_y == 0).astype(jnp.int32)
    next_split = (y_hi + last_y * (1 - 2 * y_hi)) * Z + at_z
    prev_split = (y_hi + first_y * (1 - 2 * y_hi)) * Z + at_z
    next_item = lax.rem(item + C, N_ITEM)
    prev_item = lax.rem(item + N_ITEM - C, N_ITEM)
    cross_next = lax.rem(item + 1, N_ITEM)
    cross_prev = lax.rem(item + N_ITEM - 1, N_ITEM)
    other_core = item + 1 - 2 * core

    def at_depth(d):
        return lax.rem(at_z + d, Z)

    def along_y(step, turn):
        place = lax.rem(y_hi * Y + at_y + step + 2 * Y, 2 * Y)
        peer = lax.rem(place, Y) * C + lax.rem(core + turn, C)
        return peer, (at_x * NEAR + peer, place // Y * Z + at_z)

    owner = near - C
    owns = jnp.logical_and(at_y >= 1, at_y <= 2)

    def owner_at(n, sign):
        step = lax.rem(sign * (1 + n // C - at_y) + 2 * Y, Y)
        place = lax.rem(y_hi * Y + at_y + sign * step + 2 * Y, 2 * Y)
        return at_x * NEAR + (1 + n // C) * C + n % C, place // Y * Z + at_z

    def along_x(d):
        peer = lax.rem(at_x + d, X)
        return peer, (peer * NEAR + near, split)

    barrier = pltpu.get_barrier_semaphore()

    def greet(device):
        pl.semaphore_signal(barrier, inc=1, device_id=device, device_id_type=MESH)

    for d in FAR_FIRST:
        greet((item, y_hi * Z + at_depth(d)))
    greet((item, partner))
    for step, turn in NEARBY:
        greet(along_y(-step, turn)[1])
        if step:
            greet(along_y(step, turn)[1])
    for d in range(1, X):
        greet(along_x(d)[1])
    greet((next_item, next_split))
    greet((prev_item, prev_split))

    @pl.when(core == 1)
    def _():
        greet((cross_next, next_split))

    @pl.when(core == 0)
    def _():
        greet((cross_prev, prev_split))

    loads = [
        pltpu.make_async_copy(src, dst, sem_in.at[n])
        for n, (src, dst) in enumerate(
            (
                (user_hbm, user_ref),
                (item_hbm, item_ref),
                (age_hbm, age_ref),
                (count_hbm, count_ref),
                (conf_hbm, conf_ref),
                (emb_hbm, emb_ref),
            )
        )
    ]
    for load in loads:
        load.start()

    def copy(src, dst, send_sem, recv_sem, device):
        return pltpu.make_async_remote_copy(
            src_ref=src, dst_ref=dst, send_sem=send_sem, recv_sem=recv_sem,
            device_id=device, device_id_type=MESH,
        )

    for load in loads[:4]:
        load.wait()
    spread = block_weights(user_ref[...], item_ref[...], age_ref[...], count_ref[...])
    half = USERS * 8
    row = lax.broadcasted_iota(jnp.int32, (half, 1), 0)
    row_user = row // 8
    row_code = ((row_user // 8) * 4 + lax.rem(row, 4)) * 16
    row_code = row_code + (lax.rem(row, 8) // 4) * 8 + lax.rem(row_user, 8)
    row_code = row_code.astype(F32)
    lane = lax.broadcasted_iota(jnp.int32, (1, 2 * EMB), 1)
    lane_code = (lane // EMB * 8 + lax.rem(lane, 8)).astype(F32)
    ones = jnp.ones((2 * EMB, EMB), BF16)
    rows_8 = lax.broadcasted_iota(jnp.int32, (8, EMB), 0)
    lanes_8 = lax.broadcasted_iota(jnp.int32, (8, EMB), 1)
    recency_rows = [jnp.zeros((1, EMB), F32) for _ in range(3)]
    loads[4].wait()
    for pair in range(2):
        k = 2 * pair
        recency = jnp.concatenate([spread[k : k + 1], spread[k + 1 : k + 2]], axis=1)
        code = jnp.concatenate([spread[4 + k : 5 + k], spread[5 + k : 6 + k]], axis=1)
        code = code * 16.0 + lane_code
        place = jnp.where(row_code == code, recency, 0.0)
        high, rest = high_low(place)
        low = (place - high.astype(F32) - rest.astype(F32)).astype(BF16)
        values = jnp.concatenate([conf_ref[pl.ds(2 * EMB * pair, 2 * EMB), :], ones], axis=1)
        sums = jnp.dot(
            jnp.concatenate([high, rest, low], axis=0), values, preferred_element_type=F32
        )
        sums = sums[:half] + sums[half : 2 * half] + sums[2 * half :]
        by_user = sums[:, :EMB].reshape(Z, 2, 8, EMB)
        for u in range(2):
            send_a[:, pl.ds(SLOTS * u + 8 * pair, 8), :] = by_user[:, u]
        for block in range(3):
            part = sums[64 * block : 64 * block + 8, EMB:]
            part = jnp.where(lanes_8 == rows_8 + 8 * pair, part, 0.0)
            recency_rows[block] = recency_rows[block] + jnp.sum(part, axis=0, keepdims=True)
    for peer in range(Z):
        send_a[peer, 2 * SLOTS : 2 * SLOTS + 1, :] = recency_rows[peer // 4]

    def prepare(slot, rows):
        high, low = high_low(rows)
        split_w[slot, :, pl.ds(0, EMB)] = high
        split_w[slot, :, pl.ds(EMB, EMB)] = low
        turned = rows.T
        window_t[slot] = turned
        return turned

    def three_products(left, slot):
        high, low = high_low(left)
        count = left.shape[0]
        both = jnp.concatenate([high, low], axis=0)
        out = jnp.dot(both, split_w[slot], preferred_element_type=F32)
        return out[:count, :EMB] + out[:count, EMB:] + out[count:, :EMB]

    loads[5].wait()
    turned = prepare(0, emb_ref[...])
    local_gram[...] = three_products(turned, 0).reshape(OWNERS, BLOCK, EMB)

    pl.semaphore_wait(barrier, Z - 1 + 1 + 13 + X - 1 + 3)

    def chunk(c):
        return pl.ds(c * CHUNK, CHUNK)

    def own_next(c):
        return copy(
            emb_ref.at[chunk(c)], window.at[2, chunk(c)],
            sem_ws.at[0, c], sem_wr.at[1, c], (next_item, next_split),
        )

    def own_core(c):
        return copy(
            emb_ref.at[chunk(c)], window.at[1, chunk(c)],
            sem_ws.at[1, c], sem_wr.at[0, c], (other_core, split),
        )

    def relay_core(c, slot, send_slot):
        return copy(
            window.at[2, chunk(c)], window.at[slot, chunk(c)],
            sem_ws.at[send_slot, c], sem_wr.at[slot - 1, c], (other_core, split),
        )

    def relay_next(c):
        return copy(
            window.at[2, chunk(c)], window.at[3, chunk(c)],
            sem_ws.at[2, c], sem_wr.at[2, c], (cross_next, next_split),
        )

    def pass_on(c):
        own_next(c).wait_recv()

        @pl.when(core == 1)
        def _():
            relay_next(c).start()

    def share(c):
        @pl.when(core == 0)
        def _():
            relay_core(c, 3, 2).start()

        @pl.when(core == 1)
        def _():
            relay_core(c, 1, 1).start()

    def depth_copy(d):
        peer = at_depth(d)
        return copy(
            send_a.at[peer, pl.ds(0, SENT)], recv_a.at[at_z, pl.ds(0, SENT)],
            sem_as.at[d], sem_ar.at[at_z], (item, y_hi * Z + peer),
        )

    def gram_copy_1(n):
        return copy(
            local_gram.at[n], gram_1.at[near], sem_g1s.at[n], sem_g1r.at[near], owner_at(n, -1)
        )

    def gram_copy_2(d):
        return copy(
            gram_2.at[at_x], gram_2.at[at_x], sem_g2s.at[d], sem_g2r.at[at_x], along_x(d)[1]
        )

    def gram_copy_3(n):
        device = along_y(-NEARBY[n][0], NEARBY[n][1])[1]
        return copy(
            gram_3.at[owner], gram_3.at[owner], sem_g3s.at[n], sem_g3r.at[owner], device
        )

    def for_other_owners(act):
        for n in range(OWNERS):

            @pl.when(owner != n)
            def _():
                act(n)

    for d in FAR_FIRST:
        depth_copy(d).start()
    for_other_owners(lambda n: gram_copy_1(n).start())
    for c in range(CHUNKS):
        own_next(c).start()

    @pl.when(core == 0)
    def _():
        for c in range(CHUNKS):
            own_core(c).start()

    @pl.when(owns)
    def _():
        total = local_gram[owner]
        for step, turn in NEARBY:
            peer, device = along_y(step, turn)
            copy(
                local_gram.at[0], gram_1.at[peer], sem_g1s.at[0], sem_g1r.at[peer], device
            ).wait_recv()
            total = total + gram_1[peer]
        gram_2[at_x] = total
        for d in range(1, X):
            gram_copy_2(d).start()

    pass_on(0)

    for c in range(1, CHUNKS):
        pass_on(c)

    total = send_a[at_z, pl.ds(0, SENT)]
    for d in reversed(FAR_FIRST):
        peer = at_depth(d)
        copy(
            send_a.at[0, pl.ds(0, SENT)], recv_a.at[peer, pl.ds(0, SENT)],
            sem_as.at[d], sem_ar.at[peer], (item, y_hi * Z + peer),
        ).wait_recv()
        total = total + recv_a[peer, pl.ds(0, SENT)]
    pair_a[pl.ds(0, SENT)] = total
    send_pair = copy(
        pair_a.at[pl.ds(0, SENT)], recv_b.at[pl.ds(0, SENT)], sem_bs, sem_br, (item, partner)
    )
    send_pair.start()

    for c in range(CHUNKS):
        share(c)

    @pl.when(owns)
    def _():
        for d in range(1, X):
            peer, device = along_x(d)
            copy(
                gram_2.at[peer], gram_2.at[peer], sem_g2s.at[d], sem_g2r.at[peer], device
            ).wait_recv()
        gram_3[owner] = gram_2[0] + gram_2[1] + gram_2[2] + gram_2[3]
        for n in range(NEAR - 1):
            gram_copy_3(n).start()

    prepare(2, window[2])
    for slot in (1, 3):
        for c in range(CHUNKS):
            copy(
                window.at[2, chunk(c)], window.at[slot, chunk(c)],
                sem_ws.at[0, c], sem_wr.at[slot - 1, c], (other_core, split),
            ).wait_recv()
        prepare(slot, window[slot])
    for_other_owners(
        lambda n: copy(
            gram_3.at[n], gram_3.at[n], sem_g3s.at[0], sem_g3r.at[n], owner_at(n, 1)
        ).wait_recv()
    )
    eye = lax.broadcasted_iota(jnp.int32, (EMB, EMB), 0)
    eye = eye == lax.broadcasted_iota(jnp.int32, (EMB, EMB), 1)
    base = gram_3[...].reshape(EMB, EMB) + jnp.where(eye, RIDGE, 0.0)

    send_pair.wait_recv()
    both = pair_a[pl.ds(0, SENT)] + recv_b[pl.ds(0, SENT)]
    weights = both[: 2 * SLOTS].reshape(2, SLOTS, EMB)
    block_row = jnp.broadcast_to(both[2 * SLOTS : 2 * SLOTS + 1], (SLOTS, EMB))
    rows_16 = lax.broadcasted_iota(jnp.int32, (SLOTS, EMB), 0)
    lanes_16 = lax.broadcasted_iota(jnp.int32, (SLOTS, EMB), 1)
    block_col = jnp.sum(jnp.where(rows_16 == lanes_16, block_row, 0.0), axis=1, keepdims=True)

    def weighted(slot):
        base_row = 4 * slot
        parts = []
        for u in range(2):
            wishes = weights[u] + block_col
            parts.append(
                jnp.concatenate(
                    [
                        window_t[slot, :, pl.ds(b * EMB, EMB)]
                        * weights[u, base_row + b : base_row + b + 1]
                        for b in range(4)
                    ],
                    axis=1,
                )
            )
            wish = jnp.concatenate(
                [wishes[base_row + b : base_row + b + 1] for b in range(4)], axis=1
            )
            parts.append(jnp.broadcast_to(wish, (8, ROWS)))
        return three_products(jnp.concatenate(parts, axis=0), slot)

    system = weighted(0)
    for slot in range(1, STEPS):
        system = system + weighted(slot)

    def over(value):
        return jnp.sum(value, axis=1, keepdims=True)

    stride = EMB + 8
    matrices = [system[u * stride : u * stride + EMB] + base for u in range(2)]
    right = jnp.concatenate(
        [system[u * stride + EMB : (u + 1) * stride] for u in range(2)], axis=0
    )
    answer = jnp.zeros_like(right)
    residual = right
    direction = right
    norm_now = over(residual * residual)
    pieces = [jnp.concatenate(high_low(matrix), axis=1) for matrix in matrices]
    for _ in range(CG_ITERS):
        left = jnp.concatenate(high_low(direction), axis=0)
        image = []
        for u in range(2):
            out = jnp.dot(left, pieces[u], preferred_element_type=F32)
            rows = slice(8 * u, 8 * u + 8)
            rest = slice(16 + 8 * u, 24 + 8 * u)
            image.append(out[rows, :EMB] + out[rows, EMB:] + out[rest, :EMB])
        image = jnp.concatenate(image, axis=0)
        step_size = norm_now / over(direction * image)
        answer = answer + step_size * direction
        residual = residual - step_size * image
        norm_next = over(residual * residual)
        direction = residual + (norm_next / norm_now) * direction
        norm_now = norm_next
    result[2 * at_z] = answer[:1]
    result[2 * at_z + 1] = answer[8:9]

    def answer_copy(d):
        return copy(
            result.at[pl.ds(2 * at_z, 2)], result.at[pl.ds(2 * at_z, 2)],
            sem_xs.at[d], sem_xr.at[at_z], (item, y_hi * Z + at_depth(d)),
        )

    for d in FAR_FIRST:
        answer_copy(d).start()

    for c in range(CHUNKS):
        own_next(c).wait_send()
        relay_core(c, 1, 1).wait_send()
        relay_next(c).wait_send()
    for d in range(1, Z):
        depth_copy(d).wait_send()
    send_pair.wait_send()
    for_other_owners(lambda n: gram_copy_1(n).wait_send())

    @pl.when(owns)
    def _():
        for n in range(NEAR - 1):
            gram_copy_3(n).wait_send()
        for d in range(1, X):
            gram_copy_2(d).wait_send()

    for d in range(1, Z):
        peer = at_depth(d)
        copy(
            result.at[pl.ds(2 * peer, 2)], result.at[pl.ds(2 * peer, 2)],
            sem_xs.at[d], sem_xr.at[peer], (item, y_hi * Z + peer),
        ).wait_recv()
    for d in range(1, Z):
        answer_copy(d).wait_send()
    for u in range(USERS):
        out_ref[u : u + 1, :] = result[u]


def body(item_emb, confidences, user_block, item_block, block_age, block_count):
    dma = pltpu.SemaphoreType.DMA
    hbm = pl.BlockSpec(memory_space=pltpu.HBM)
    def hold(value):
        return pltpu.with_memory_space_constraint(value, pltpu.HBM)

    return pl.pallas_call(
        kernel,
        out_shape=jax.ShapeDtypeStruct((USERS, EMB), F32),
        in_specs=[hbm] * 6,
        out_specs=pl.BlockSpec(memory_space=pltpu.VMEM),
        scratch_shapes=[
            pltpu.VMEM((ROWS, EMB), F32),
            pltpu.VMEM((ROWS, EMB), BF16),
            pltpu.VMEM((STEPS, SLOTS), jnp.int32),
            pltpu.VMEM((STEPS, SLOTS), jnp.int32),
            pltpu.VMEM((STEPS, SLOTS), jnp.int32),
            pltpu.VMEM((1, STEPS), jnp.int32),
            pltpu.VMEM((Z, HELD, EMB), F32),
            pltpu.VMEM((Z, HELD, EMB), F32),
            pltpu.VMEM((HELD, EMB), F32),
            pltpu.VMEM((HELD, EMB), F32),
            pltpu.VMEM((STEPS, ROWS, EMB), F32),
            pltpu.VMEM((STEPS, EMB, ROWS), F32),
            pltpu.VMEM((STEPS, ROWS, 2 * EMB), BF16),
            pltpu.VMEM((OWNERS, BLOCK, EMB), F32),
            pltpu.VMEM((NEAR, BLOCK, EMB), F32),
            pltpu.VMEM((X, BLOCK, EMB), F32),
            pltpu.VMEM((OWNERS, BLOCK, EMB), F32),
            pltpu.VMEM((USERS, 1, EMB), F32),
            dma((6,)), dma((Z,)), dma((Z,)), dma(()), dma(()),
            dma((3, CHUNKS)), dma((3, CHUNKS)),
            dma((OWNERS,)), dma((NEAR,)), dma((X,)), dma((X,)), dma((NEAR,)), dma((OWNERS,)),
            dma((Z,)), dma((Z,)),
        ],
        compiler_params=pltpu.CompilerParams(
            collective_id=0, has_side_effects=True, vmem_limit_bytes=32 << 20
        ),
        name="als_half_sweep",
    )(
        hold(item_emb),
        hold(confidences.reshape(ROWS, EMB)),
        hold(user_block.reshape(STEPS, SLOTS)),
        hold(item_block.reshape(STEPS, SLOTS)),
        hold(block_age.reshape(STEPS, SLOTS)),
        hold(block_count.reshape(1, STEPS)),
    )


def solution(mesh):
    placed = (
        P("item", None),
        P("item", "split", None, None, None, None),
        P("item", "split", None, None),
        P("item", "split", None, None),
        P("item", "split", None, None),
        P("item", "split", None),
    )
    return jax.shard_map(
        body, mesh=mesh, in_specs=placed, out_specs=P("item", None), check_vma=False
    )
```

```python
import jax
import jax.numpy as jnp
from jax import lax
from jax.experimental import pallas as pl
from jax.experimental.pallas import tpu as pltpu
from jax.sharding import PartitionSpec as P

CG_ITERS = 3
STEPS = 4
SLOTS = 16
USERS = 24
EMB = 128
ROWS = 512
X, Y, C = 4, 4, 2
N_ITEM = X * Y * C
Z = 12
NEAR = Y * C
OWNERS = 2 * C
BLOCK = EMB // OWNERS
NEARBY = ((3, 0), (3, 1), (2, 0), (2, 1), (1, 0), (1, 1), (0, 1))
CHUNKS = 2
CHUNK = ROWS // CHUNKS
RIDGE = 0.1
HELD = 40
SENT = 33
FAR_FIRST = (6, 5, 7, 4, 8, 3, 9, 2, 10, 1, 11)
F32 = jnp.float32
BF16 = jnp.bfloat16
MESH = pl.DeviceIdType.MESH


def high_low(value):
    high = value.astype(BF16)
    return high, (value - high.astype(F32)).astype(BF16)


def block_weights(user_block, item_block, block_age, block_count):
    lane = lax.broadcasted_iota(jnp.int32, (STEPS, SLOTS), 1)
    row = lax.broadcasted_iota(jnp.int32, (STEPS, STEPS), 0)
    col = lax.broadcasted_iota(jnp.int32, (STEPS, STEPS), 1)
    counts = jnp.broadcast_to(block_count.astype(F32), (STEPS, STEPS))
    counts = jnp.sum(jnp.where(row == col, counts, 0.0), axis=1, keepdims=True)
    recency = 2.0 / (2.0 + block_age.astype(F32))
    recency = jnp.where(lane.astype(F32) < counts, recency, 0.0)
    code = (user_block * 4 + item_block).astype(F32)
    both = jnp.concatenate([recency, code], axis=0)
    slot = lax.broadcasted_iota(jnp.int32, (SLOTS, EMB), 0)
    spread = lax.broadcasted_iota(jnp.int32, (SLOTS, EMB), 1) // 8
    spread = jnp.where(slot == spread, 1.0, 0.0).astype(F32)
    return jnp.dot(both, spread, precision=lax.Precision.HIGHEST, preferred_element_type=F32)


def kernel(
    emb_hbm, conf_hbm, user_hbm, item_hbm, age_hbm, count_hbm, out_ref,
    emb_ref, conf_ref, user_ref, item_ref, age_ref, count_ref,
    send_a, recv_a, pair_a, recv_b,
    window, window_t, split_w, local_gram, gram_1, gram_2, gram_3, result,
    sem_in, sem_as, sem_ar, sem_bs, sem_br,
    sem_ws, sem_wr, sem_g1s, sem_g1r, sem_g2s, sem_g2r, sem_g3s, sem_g3r,
    sem_xs, sem_xr,
):
    item = lax.axis_index("item")
    split = lax.axis_index("split")
    core = lax.rem(item, C)
    near = lax.rem(item, NEAR)
    at_x = item // NEAR
    at_y = near // C
    y_hi = split // Z
    at_z = lax.rem(split, Z)
    partner = (1 - y_hi) * Z + at_z
    last_y = (at_y == Y - 1).astype(jnp.int32)
    first_y = (at_y == 0).astype(jnp.int32)
    next_split = (y_hi + last_y * (1 - 2 * y_hi)) * Z + at_z
    prev_split = (y_hi + first_y * (1 - 2 * y_hi)) * Z + at_z
    next_item = lax.rem(item + C, N_ITEM)
    prev_item = lax.rem(item + N_ITEM - C, N_ITEM)
    cross_next = lax.rem(item + 1, N_ITEM)
    cross_prev = lax.rem(item + N_ITEM - 1, N_ITEM)
    other_core = item + 1 - 2 * core

    def at_depth(d):
        return lax.rem(at_z + d, Z)

    def along_y(step, turn):
        place = lax.rem(y_hi * Y + at_y + step + 2 * Y, 2 * Y)
        peer = lax.rem(place, Y) * C + lax.rem(core + turn, C)
        return peer, (at_x * NEAR + peer, place // Y * Z + at_z)

    owner = near - C
    owns = jnp.logical_and(at_y >= 1, at_y <= 2)

    def owner_at(n, sign):
        step = lax.rem(sign * (1 + n // C - at_y) + 2 * Y, Y)
        place = lax.rem(y_hi * Y + at_y + sign * step + 2 * Y, 2 * Y)
        return at_x * NEAR + (1 + n // C) * C + n % C, place // Y * Z + at_z

    def along_x(d):
        peer = lax.rem(at_x + d, X)
        return peer, (peer * NEAR + near, split)

    barrier = pltpu.get_barrier_semaphore()

    def greet(device):
        pl.semaphore_signal(barrier, inc=1, device_id=device, device_id_type=MESH)

    for d in FAR_FIRST:
        greet((item, y_hi * Z + at_depth(d)))
    greet((item, partner))
    for step, turn in NEARBY:
        greet(along_y(-step, turn)[1])
        if step:
            greet(along_y(step, turn)[1])
    for d in range(1, X):
        greet(along_x(d)[1])
    greet((next_item, next_split))
    greet((prev_item, prev_split))

    @pl.when(core == 1)
    def _():
        greet((cross_next, next_split))

    @pl.when(core == 0)
    def _():
        greet((cross_prev, prev_split))

    loads = [
        pltpu.make_async_copy(src, dst, sem_in.at[n])
        for n, (src, dst) in enumerate(
            (
                (user_hbm, user_ref),
                (item_hbm, item_ref),
                (age_hbm, age_ref),
                (count_hbm, count_ref),
                (conf_hbm, conf_ref),
                (emb_hbm, emb_ref),
            )
        )
    ]
    for load in loads:
        load.start()

    def copy(src, dst, send_sem, recv_sem, device):
        return pltpu.make_async_remote_copy(
            src_ref=src, dst_ref=dst, send_sem=send_sem, recv_sem=recv_sem,
            device_id=device, device_id_type=MESH,
        )

    for load in loads[:4]:
        load.wait()
    spread = block_weights(user_ref[...], item_ref[...], age_ref[...], count_ref[...])
    half = USERS * 8
    row = lax.broadcasted_iota(jnp.int32, (half, 1), 0)
    row_user = row // 8
    row_code = ((row_user // 8) * 4 + lax.rem(row, 4)) * 16
    row_code = row_code + (lax.rem(row, 8) // 4) * 8 + lax.rem(row_user, 8)
    row_code = row_code.astype(F32)
    lane = lax.broadcasted_iota(jnp.int32, (1, 2 * EMB), 1)
    lane_code = (lane // EMB * 8 + lax.rem(lane, 8)).astype(F32)
    ones = jnp.ones((2 * EMB, EMB), BF16)
    rows_8 = lax.broadcasted_iota(jnp.int32, (8, EMB), 0)
    lanes_8 = lax.broadcasted_iota(jnp.int32, (8, EMB), 1)
    recency_rows = [jnp.zeros((1, EMB), F32) for _ in range(3)]
    loads[4].wait()
    for pair in range(2):
        k = 2 * pair
        recency = jnp.concatenate([spread[k : k + 1], spread[k + 1 : k + 2]], axis=1)
        code = jnp.concatenate([spread[4 + k : 5 + k], spread[5 + k : 6 + k]], axis=1)
        code = code * 16.0 + lane_code
        place = jnp.where(row_code == code, recency, 0.0)
        high, rest = high_low(place)
        low = (place - high.astype(F32) - rest.astype(F32)).astype(BF16)
        values = jnp.concatenate([conf_ref[pl.ds(2 * EMB * pair, 2 * EMB), :], ones], axis=1)
        sums = jnp.dot(
            jnp.concatenate([high, rest, low], axis=0), values, preferred_element_type=F32
        )
        sums = sums[:half] + sums[half : 2 * half] + sums[2 * half :]
        by_user = sums[:, :EMB].reshape(Z, 2, 8, EMB)
        for u in range(2):
            send_a[:, pl.ds(SLOTS * u + 8 * pair, 8), :] = by_user[:, u]
        for block in range(3):
            part = sums[64 * block : 64 * block + 8, EMB:]
            part = jnp.where(lanes_8 == rows_8 + 8 * pair, part, 0.0)
            recency_rows[block] = recency_rows[block] + jnp.sum(part, axis=0, keepdims=True)
    for peer in range(Z):
        send_a[peer, 2 * SLOTS : 2 * SLOTS + 1, :] = recency_rows[peer // 4]

    def prepare(slot, rows):
        high, low = high_low(rows)
        split_w[slot, :, pl.ds(0, EMB)] = high
        split_w[slot, :, pl.ds(EMB, EMB)] = low
        turned = rows.T
        window_t[slot] = turned
        return turned

    def three_products(left, slot):
        high, low = high_low(left)
        count = left.shape[0]
        both = jnp.concatenate([high, low], axis=0)
        out = jnp.dot(both, split_w[slot], preferred_element_type=F32)
        return out[:count, :EMB] + out[:count, EMB:] + out[count:, :EMB]

    loads[5].wait()
    turned = prepare(0, emb_ref[...])
    local_gram[...] = three_products(turned, 0).reshape(OWNERS, BLOCK, EMB)

    pl.semaphore_wait(barrier, Z - 1 + 1 + 13 + X - 1 + 3)

    def chunk(c):
        return pl.ds(c * CHUNK, CHUNK)

    def own_next(c):
        return copy(
            emb_ref.at[chunk(c)], window.at[2, chunk(c)],
            sem_ws.at[0, c], sem_wr.at[1, c], (next_item, next_split),
        )

    def own_core(c):
        return copy(
            emb_ref.at[chunk(c)], window.at[1, chunk(c)],
            sem_ws.at[1, c], sem_wr.at[0, c], (other_core, split),
        )

    def relay_core(c, slot, send_slot):
        return copy(
            window.at[2, chunk(c)], window.at[slot, chunk(c)],
            sem_ws.at[send_slot, c], sem_wr.at[slot - 1, c], (other_core, split),
        )

    def relay_next(c):
        return copy(
            window.at[2, chunk(c)], window.at[3, chunk(c)],
            sem_ws.at[2, c], sem_wr.at[2, c], (cross_next, next_split),
        )

    def pass_on(c):
        @pl.when(core == 1)
        def _():
            own_next(c).wait_recv()
            relay_next(c).start()

    def share(c):
        @pl.when(core == 0)
        def _():
            own_next(c).wait_recv()
            relay_core(c, 3, 2).start()

        @pl.when(core == 1)
        def _():
            relay_core(c, 1, 1).start()

    def depth_copy(d):
        peer = at_depth(d)
        return copy(
            send_a.at[peer, pl.ds(0, SENT)], recv_a.at[at_z, pl.ds(0, SENT)],
            sem_as.at[d], sem_ar.at[at_z], (item, y_hi * Z + peer),
        )

    def gram_copy_1(n):
        return copy(
            local_gram.at[n], gram_1.at[near], sem_g1s.at[n], sem_g1r.at[near], owner_at(n, -1)
        )

    def gram_copy_2(d):
        return copy(
            gram_2.at[at_x], gram_2.at[at_x], sem_g2s.at[d], sem_g2r.at[at_x], along_x(d)[1]
        )

    def gram_copy_3(n):
        device = along_y(-NEARBY[n][0], NEARBY[n][1])[1]
        return copy(
            gram_3.at[owner], gram_3.at[owner], sem_g3s.at[n], sem_g3r.at[owner], device
        )

    def for_other_owners(act):
        for n in range(OWNERS):

            @pl.when(owner != n)
            def _():
                act(n)

    for d in FAR_FIRST:
        depth_copy(d).start()
    for_other_owners(lambda n: gram_copy_1(n).start())
    for c in range(CHUNKS):
        own_next(c).start()

    @pl.when(core == 0)
    def _():
        for c in range(CHUNKS):
            own_core(c).start()

    @pl.when(owns)
    def _():
        total = local_gram[owner]
        for step, turn in NEARBY:
            peer, device = along_y(step, turn)
            copy(
                local_gram.at[0], gram_1.at[peer], sem_g1s.at[0], sem_g1r.at[peer], device
            ).wait_recv()
            total = total + gram_1[peer]
        gram_2[at_x] = total
        for d in range(1, X):
            gram_copy_2(d).start()

    pass_on(0)

    for c in range(1, CHUNKS):
        pass_on(c)

    total = send_a[at_z, pl.ds(0, SENT)]
    for d in reversed(FAR_FIRST):
        peer = at_depth(d)
        copy(
            send_a.at[0, pl.ds(0, SENT)], recv_a.at[peer, pl.ds(0, SENT)],
            sem_as.at[d], sem_ar.at[peer], (item, y_hi * Z + peer),
        ).wait_recv()
        total = total + recv_a[peer, pl.ds(0, SENT)]
    pair_a[pl.ds(0, SENT)] = total
    send_pair = copy(
        pair_a.at[pl.ds(0, SENT)], recv_b.at[pl.ds(0, SENT)], sem_bs, sem_br, (item, partner)
    )
    send_pair.start()

    for c in range(CHUNKS):
        share(c)

    @pl.when(owns)
    def _():
        for d in range(1, X):
            peer, device = along_x(d)
            copy(
                gram_2.at[peer], gram_2.at[peer], sem_g2s.at[d], sem_g2r.at[peer], device
            ).wait_recv()
        gram_3[owner] = gram_2[0] + gram_2[1] + gram_2[2] + gram_2[3]
        for n in range(NEAR - 1):
            gram_copy_3(n).start()

    prepare(2, window[2])
    for slot in (1, 3):
        for c in range(CHUNKS):
            copy(
                window.at[2, chunk(c)], window.at[slot, chunk(c)],
                sem_ws.at[0, c], sem_wr.at[slot - 1, c], (other_core, split),
            ).wait_recv()
        prepare(slot, window[slot])
    for_other_owners(
        lambda n: copy(
            gram_3.at[n], gram_3.at[n], sem_g3s.at[0], sem_g3r.at[n], owner_at(n, 1)
        ).wait_recv()
    )
    eye = lax.broadcasted_iota(jnp.int32, (EMB, EMB), 0)
    eye = eye == lax.broadcasted_iota(jnp.int32, (EMB, EMB), 1)
    base = gram_3[...].reshape(EMB, EMB) + jnp.where(eye, RIDGE, 0.0)

    send_pair.wait_recv()
    both = pair_a[pl.ds(0, SENT)] + recv_b[pl.ds(0, SENT)]
    weights = both[: 2 * SLOTS].reshape(2, SLOTS, EMB)
    block_row = jnp.broadcast_to(both[2 * SLOTS : 2 * SLOTS + 1], (SLOTS, EMB))
    rows_16 = lax.broadcasted_iota(jnp.int32, (SLOTS, EMB), 0)
    lanes_16 = lax.broadcasted_iota(jnp.int32, (SLOTS, EMB), 1)
    block_col = jnp.sum(jnp.where(rows_16 == lanes_16, block_row, 0.0), axis=1, keepdims=True)

    def weighted(slot):
        base_row = 4 * slot
        parts = []
        for u in range(2):
            wishes = weights[u] + block_col
            parts.append(
                jnp.concatenate(
                    [
                        window_t[slot, :, pl.ds(b * EMB, EMB)]
                        * weights[u, base_row + b : base_row + b + 1]
                        for b in range(4)
                    ],
                    axis=1,
                )
            )
            wish = jnp.concatenate(
                [wishes[base_row + b : base_row + b + 1] for b in range(4)], axis=1
            )
            parts.append(jnp.broadcast_to(wish, (8, ROWS)))
        return three_products(jnp.concatenate(parts, axis=0), slot)

    system = weighted(0)
    for slot in range(1, STEPS):
        system = system + weighted(slot)

    def over(value):
        return jnp.sum(value, axis=1, keepdims=True)

    stride = EMB + 8
    matrices = [system[u * stride : u * stride + EMB] + base for u in range(2)]
    right = jnp.concatenate(
        [system[u * stride + EMB : (u + 1) * stride] for u in range(2)], axis=0
    )
    answer = jnp.zeros_like(right)
    residual = right
    direction = right
    norm_now = over(residual * residual)
    pieces = [jnp.concatenate(high_low(matrix), axis=1) for matrix in matrices]
    for _ in range(CG_ITERS):
        left = jnp.concatenate(high_low(direction), axis=0)
        image = []
        for u in range(2):
            out = jnp.dot(left, pieces[u], preferred_element_type=F32)
            rows = slice(8 * u, 8 * u + 8)
            rest = slice(16 + 8 * u, 24 + 8 * u)
            image.append(out[rows, :EMB] + out[rows, EMB:] + out[rest, :EMB])
        image = jnp.concatenate(image, axis=0)
        step_size = norm_now / over(direction * image)
        answer = answer + step_size * direction
        residual = residual - step_size * image
        norm_next = over(residual * residual)
        direction = residual + (norm_next / norm_now) * direction
        norm_now = norm_next
    result[2 * at_z] = answer[:1]
    result[2 * at_z + 1] = answer[8:9]

    def answer_copy(d):
        return copy(
            result.at[pl.ds(2 * at_z, 2)], result.at[pl.ds(2 * at_z, 2)],
            sem_xs.at[d], sem_xr.at[at_z], (item, y_hi * Z + at_depth(d)),
        )

    for d in FAR_FIRST:
        answer_copy(d).start()

    for c in range(CHUNKS):
        own_next(c).wait_send()
        relay_core(c, 1, 1).wait_send()
        relay_next(c).wait_send()
    for d in range(1, Z):
        depth_copy(d).wait_send()
    send_pair.wait_send()
    for_other_owners(lambda n: gram_copy_1(n).wait_send())

    @pl.when(owns)
    def _():
        for n in range(NEAR - 1):
            gram_copy_3(n).wait_send()
        for d in range(1, X):
            gram_copy_2(d).wait_send()

    for d in range(1, Z):
        peer = at_depth(d)
        copy(
            result.at[pl.ds(2 * peer, 2)], result.at[pl.ds(2 * peer, 2)],
            sem_xs.at[d], sem_xr.at[peer], (item, y_hi * Z + peer),
        ).wait_recv()
    for d in range(1, Z):
        answer_copy(d).wait_send()
    for u in range(USERS):
        out_ref[u : u + 1, :] = result[u]


def body(item_emb, confidences, user_block, item_block, block_age, block_count):
    dma = pltpu.SemaphoreType.DMA
    hbm = pl.BlockSpec(memory_space=pltpu.HBM)
    def hold(value):
        return pltpu.with_memory_space_constraint(value, pltpu.HBM)

    return pl.pallas_call(
        kernel,
        out_shape=jax.ShapeDtypeStruct((USERS, EMB), F32),
        in_specs=[hbm] * 6,
        out_specs=pl.BlockSpec(memory_space=pltpu.VMEM),
        scratch_shapes=[
            pltpu.VMEM((ROWS, EMB), F32),
            pltpu.VMEM((ROWS, EMB), BF16),
            pltpu.VMEM((STEPS, SLOTS), jnp.int32),
            pltpu.VMEM((STEPS, SLOTS), jnp.int32),
            pltpu.VMEM((STEPS, SLOTS), jnp.int32),
            pltpu.VMEM((1, STEPS), jnp.int32),
            pltpu.VMEM((Z, HELD, EMB), F32),
            pltpu.VMEM((Z, HELD, EMB), F32),
            pltpu.VMEM((HELD, EMB), F32),
            pltpu.VMEM((HELD, EMB), F32),
            pltpu.VMEM((STEPS, ROWS, EMB), F32),
            pltpu.VMEM((STEPS, EMB, ROWS), F32),
            pltpu.VMEM((STEPS, ROWS, 2 * EMB), BF16),
            pltpu.VMEM((OWNERS, BLOCK, EMB), F32),
            pltpu.VMEM((NEAR, BLOCK, EMB), F32),
            pltpu.VMEM((X, BLOCK, EMB), F32),
            pltpu.VMEM((OWNERS, BLOCK, EMB), F32),
            pltpu.VMEM((USERS, 1, EMB), F32),
            dma((6,)), dma((Z,)), dma((Z,)), dma(()), dma(()),
            dma((3, CHUNKS)), dma((3, CHUNKS)),
            dma((OWNERS,)), dma((NEAR,)), dma((X,)), dma((X,)), dma((NEAR,)), dma((OWNERS,)),
            dma((Z,)), dma((Z,)),
        ],
        compiler_params=pltpu.CompilerParams(
            collective_id=0, has_side_effects=True, vmem_limit_bytes=32 << 20
        ),
        name="als_half_sweep",
    )(
        hold(item_emb),
        hold(confidences.reshape(ROWS, EMB)),
        hold(user_block.reshape(STEPS, SLOTS)),
        hold(item_block.reshape(STEPS, SLOTS)),
        hold(block_age.reshape(STEPS, SLOTS)),
        hold(block_count.reshape(1, STEPS)),
    )


def solution(mesh):
    placed = (
        P("item", None),
        P("item", "split", None, None, None, None),
        P("item", "split", None, None),
        P("item", "split", None, None),
        P("item", "split", None, None),
        P("item", "split", None),
    )
    return jax.shard_map(
        body, mesh=mesh, in_specs=placed, out_specs=P("item", None), check_vma=False
    )
```
